32 devices in a mesh: row: 8 (over y, x, core), col: 4 (over z).
Axes of the slice: x: 2, y: 2, z: 4, core: 2. Of those that a mesh axis runs over, the one named last changes fastest.
Arguments:
- pair: bfloat16 [256, 256, 128], P('row', 'col'), may hold values from -6 to 6
- cotangent: bfloat16 [256, 256, 128], P('row', 'col'), may hold values from -6 to 6
- length: int32 [1], replicated, may hold values from 128 to 256
- norm_gain: float32 [128], replicated, may hold values from 0.1 to 1.9
- norm_bias: float32 [128], replicated, may hold values from -1.5 to 1.5
- left_weight: bfloat16 [128, 256], replicated, may hold values from -0.5 to 0.5
- right_weight: bfloat16 [128, 256], replicated, may hold values from -0.5 to 0.5
- gate_weight: bfloat16 [128, 128], replicated, may hold values from -0.5 to 0.5
- out_gain: float32 [128], replicated, may hold values from 0.1 to 1.9
- out_bias: float32 [128], replicated, may hold values from -2 to 2
- out_weight: bfloat16 [128, 128], replicated, may hold values from -0.5 to 0.5
Outputs:
- update: bfloat16 [256, 256, 128], P('row', 'col')
- grad_pair: bfloat16 [256, 256, 128], P('row', 'col')
- grad_left: float32 [128, 256], replicated
- grad_right: float32 [128, 256], replicated
- grad_gating: float32 [128, 128], replicated
- grad_output: float32 [128, 128], replicated
- grad_norms: float32 [4, 128], replicated
The draws below stay inside these ranges and needn't reach their ends.
Inputs may be any that keep to these rules, and one draw needn't show every extreme that they name: Tokens at positions 255 down to length are padding.
All inputs are finite; a program needn't handle non-finite values.
Results may differ from the reference program's by a relative error of at most 0.014.
Values may be sent and summed in bfloat16 or wider, within the bound.
No kernel may reach another device: no remote copies, remote signals or barrier semaphores. Data moves between devices by JAX's collectives and lax.ppermute only.
A program may use at most 128 MiB of HBM per device.

```python
import jax
import jax.numpy as jnp
from jax import lax

PAIR = 128
HIDDEN_SIZE = 128
ROW_DEV = 32
TOKENS = 256
COL_DEV = 64
N_ROW = 8
N_COL = 4


def shard_levels(rng, shape, split, smallest, high):
    level, own = 1.0, jax.random.fold_in(rng, 6)
    for position, parts in split:
        draws = jnp.exp(jax.random.uniform(jax.random.fold_in(own, position), (parts,), jnp.float32, smallest / len(split), high / len(split)))
        level = level * jnp.repeat(draws, shape[position] // parts).reshape([-1 if axis == position else 1 for axis in range(len(shape))])
    return level


def normal_values(rng, dims, scale, bound, split=(), kind=jnp.bfloat16):
    entries = jax.random.normal(rng, dims, jnp.float32) * scale
    if len(split) > 0:
        entries = shard_levels(rng, dims, split, -0.22, 0.18) * entries
    return jnp.clip(entries, min=-bound, max=bound).astype(kind)


def setup_inputs(seed: int = 0) -> dict:
    key_list = jax.random.split(jax.random.key(seed), 12)
    pair = normal_values(key_list[0], (TOKENS, TOKENS, PAIR), 1.0, 6.0, ((0, 8), (1, 4)))
    cotangent = normal_values(key_list[1], (TOKENS, TOKENS, PAIR), 1.0, 6.0, ((0, 8), (1, 4)))
    length = jax.random.randint(key_list[2], (1,), TOKENS // 2, TOKENS + 1).astype(jnp.int32)
    norm_gain = jnp.clip(1.0 + 0.18 * jax.random.normal(key_list[3], (PAIR,), jnp.float32), 0.1, 1.9)
    norm_bias = normal_values(key_list[4], (PAIR,), 0.3, 1.5, (), jnp.float32)
    left_weight = normal_values(key_list[5], (PAIR, 2 * HIDDEN_SIZE), PAIR ** -0.5, 0.5)
    right_weight = normal_values(key_list[6], (PAIR, 2 * HIDDEN_SIZE), PAIR ** -0.5, 0.5)
    gate_weight = normal_values(key_list[7], (PAIR, PAIR), PAIR ** -0.5, 0.5)
    out_gain = jnp.clip(1.0 + 0.18 * jax.random.normal(key_list[8], (HIDDEN_SIZE,), jnp.float32), 0.1, 1.9)
    out_bias = normal_values(key_list[9], (HIDDEN_SIZE,), 0.5, 2.0, (), jnp.float32)
    out_weight = normal_values(key_list[10], (HIDDEN_SIZE, PAIR), HIDDEN_SIZE ** -0.5, 0.5)
    return dict(pair=pair, cotangent=cotangent, length=length, norm_gain=norm_gain, norm_bias=norm_bias, left_weight=left_weight, right_weight=right_weight, gate_weight=gate_weight, out_gain=out_gain, out_bias=out_bias, out_weight=out_weight)


EPS = 1e-05

def normalize(values):
    center = values - lax.optimization_barrier(jnp.mean(values, axis=-1, keepdims=True))
    inverse = lax.rsqrt(lax.optimization_barrier(jnp.mean(center * center, axis=-1, keepdims=True)) + EPS)
    return (center * inverse, inverse)

def product(form, first, second):
    return jnp.einsum(form, first.astype(jnp.float32), second.astype(jnp.float32), precision=lax.Precision.HIGHEST)

def rounded(values):
    return lax.optimization_barrier(values.astype(jnp.bfloat16)).astype(jnp.float32)

def reference(pair, cotangent, length, norm_gain, norm_bias, left_weight, right_weight, gate_weight, out_gain, out_bias, out_weight):
    pair_hat, pair_scale = normalize(pair.astype(jnp.float32))
    normed = (pair_hat * norm_gain + norm_bias).astype(jnp.bfloat16)
    valid = (jnp.arange(TOKENS, dtype=jnp.int32) < length[0]).astype(jnp.float32)
    pad_mask = (valid[:, None] * valid[None, :])[..., None]

    def gating(weight):
        projected = product('ikc,ch->ikh', normed, weight)
        values = projected[..., :HIDDEN_SIZE]
        sigmoid_val = jax.nn.sigmoid(projected[..., HIDDEN_SIZE:])
        return ((pad_mask * sigmoid_val * values).astype(jnp.bfloat16), values, sigmoid_val)
    left_act, left_val, left_sig = gating(left_weight)
    right_act, right_val, right_sig = gating(right_weight)
    tri = product('ikh,jkh->ijh', left_act, right_act)
    tri_hat, tri_scale = normalize(tri)
    tri_normed = (tri_hat * out_gain + out_bias).astype(jnp.bfloat16)
    outer_val = product('ijh,hc->ijc', tri_normed, out_weight)
    gate_val = jax.nn.sigmoid(product('ijc,cd->ijd', normed, gate_weight))
    update = (gate_val * outer_val).astype(jnp.bfloat16)
    upstream = cotangent.astype(jnp.float32)
    outer_grad = (upstream * gate_val).astype(jnp.bfloat16)
    gate_grad = (upstream * outer_val * gate_val * (1.0 - gate_val)).astype(jnp.bfloat16)
    grad_output = product('ijh,ijc->hc', tri_normed, outer_grad)
    grad_gating = product('ijc,ijd->cd', normed, gate_grad)
    tnorm_grad = product('ijc,hc->ijh', outer_grad, out_weight)
    hat_grad = tnorm_grad * out_gain
    tri_grad = (tri_scale * (hat_grad - lax.optimization_barrier(jnp.mean(hat_grad, axis=-1, keepdims=True)) - tri_hat * lax.optimization_barrier(jnp.mean(hat_grad * tri_hat, axis=-1, keepdims=True)))).astype(jnp.bfloat16)
    row_part = jnp.zeros((TOKENS, TOKENS, HIDDEN_SIZE), jnp.float32)
    for column in range(N_COL):
        lower = column * COL_DEV
        row_part = row_part + rounded(product('ijh,jkh->ikh', tri_grad[:, lower:lower + COL_DEV], right_act[lower:lower + COL_DEV]))
    col_part = jnp.zeros((TOKENS, TOKENS, HIDDEN_SIZE), jnp.float32)
    for row_block in range(N_ROW):
        lower = row_block * ROW_DEV
        col_part = col_part + rounded(product('ijh,ikh->jkh', tri_grad[lower:lower + ROW_DEV], left_act[lower:lower + ROW_DEV]))
    col_part = rounded(col_part)

    def push_back(partial_value, values, sigmoid_val, weight):
        combined = jnp.concatenate([partial_value * pad_mask * sigmoid_val, partial_value * pad_mask * values * sigmoid_val * (1.0 - sigmoid_val)], axis=-1).astype(jnp.bfloat16)
        return (product('ikh,ch->ikc', combined, weight), product('ikc,ikh->ch', normed, combined))
    from_rows, grad_left = push_back(row_part, left_val, left_sig, left_weight)
    from_cols, grad_right = push_back(col_part, right_val, right_sig, right_weight)
    normed_grad = product('ijd,cd->ijc', gate_grad, gate_weight) + from_rows + from_cols
    scaled = normed_grad * norm_gain
    grad_pair = (pair_scale * (scaled - lax.optimization_barrier(jnp.mean(scaled, axis=-1, keepdims=True)) - pair_hat * lax.optimization_barrier(jnp.mean(scaled * pair_hat, axis=-1, keepdims=True)))).astype(jnp.bfloat16)
    grad_norms = jnp.stack([lax.optimization_barrier(jnp.sum(normed_grad * pair_hat, axis=(0, 1))), lax.optimization_barrier(jnp.sum(normed_grad, axis=(0, 1))), lax.optimization_barrier(jnp.sum(tnorm_grad * tri_hat, axis=(0, 1))), lax.optimization_barrier(jnp.sum(tnorm_grad, axis=(0, 1)))])
    inverse = 1.0 / TOKENS
    return (update, grad_pair, grad_left * inverse, grad_right * inverse, grad_gating * inverse, grad_output * inverse, grad_norms * inverse)
```

```python
import jax
import jax.numpy as jnp
from jax import lax
from jax.sharding import PartitionSpec as P

EPS = 1e-05
BOTH = ("row", "col")
LANES = 128


def normalize(values):
    center = values - jnp.mean(values, axis=-1, keepdims=True)
    inverse = lax.rsqrt(jnp.mean(center * center, axis=-1, keepdims=True) + EPS)
    return (center * inverse, inverse)


def exchange(blocks):
    return lax.all_to_all(blocks, BOTH, split_axis=0, concat_axis=0, tiled=True)


def total_sum(values, n_dev):
    rows = values.shape[0]
    step = 8 * n_dev
    padded = -(-rows // step) * step
    values = jnp.pad(values, ((0, padded - rows), (0, 0)))
    parts = exchange(values.reshape(n_dev, padded // n_dev, LANES))
    mine = jnp.sum(parts, axis=0)
    gathered = exchange(jnp.broadcast_to(mine[None], (n_dev,) + mine.shape))
    return gathered.reshape(padded, LANES)[:rows]


def per_device(
    pair,
    cotangent,
    length,
    norm_gain,
    norm_bias,
    left_weight,
    right_weight,
    gate_weight,
    out_gain,
    out_bias,
    out_weight,
):
    row_index = lax.axis_index("row")
    col_index = lax.axis_index("col")
    n_row = lax.axis_size("row")
    n_col = lax.axis_size("col")
    n_dev = n_row * n_col
    rows_dev, cols_dev, channels = pair.shape
    tokens = rows_dev * n_row
    hidden = out_weight.shape[0]
    own = hidden // n_dev
    f32, bf16 = jnp.float32, jnp.bfloat16

    pair_hat, pair_scale = normalize(pair.astype(f32))
    normed = (pair_hat * norm_gain + norm_bias).astype(bf16)
    real_count = length[0]
    row_ok = row_index * rows_dev + jnp.arange(rows_dev, dtype=jnp.int32) < real_count
    col_ok = col_index * cols_dev + jnp.arange(cols_dev, dtype=jnp.int32) < real_count
    mask = (row_ok[:, None] & col_ok[None, :]).astype(f32)

    def gating(weight):
        projected = jnp.einsum("ch,ikc->hik", weight, normed, preferred_element_type=f32)
        values = projected[:hidden]
        sig = jax.nn.sigmoid(projected[hidden:])
        return (mask[None] * sig * values).astype(bf16), values, sig

    left, left_val, left_sig = gating(left_weight)
    right, right_val, right_sig = gating(right_weight)

    def to_channels(tile):
        return tile.reshape(n_dev, own, rows_dev * cols_dev // LANES, LANES)

    def whole(block):
        block = block.reshape(n_row, n_col, own, rows_dev, cols_dev)
        return block.transpose(2, 0, 3, 1, 4).reshape(own, tokens, n_col * cols_dev)

    def tiles(array):
        array = array.astype(bf16).reshape(own, n_row, rows_dev, n_col, cols_dev)
        return array.transpose(1, 3, 0, 2, 4).reshape(
            n_dev, own, rows_dev * cols_dev // LANES, LANES
        )

    both = exchange(jnp.stack([to_channels(left), to_channels(right)], axis=1))
    left_all, right_all = whole(both[:, 0]), whole(both[:, 1])
    tri_own = jnp.einsum("hik,hjk->hij", left_all, right_all, preferred_element_type=f32)
    tri = exchange(tiles(tri_own)).reshape(hidden, rows_dev, cols_dev)
    tri = tri.transpose(1, 2, 0).astype(f32)

    tri_hat, tri_scale = normalize(tri)
    tri_normed = (tri_hat * out_gain + out_bias).astype(bf16)
    outer_val = jnp.einsum("ijh,hc->ijc", tri_normed, out_weight, preferred_element_type=f32)
    gate_val = jax.nn.sigmoid(
        jnp.einsum("ijc,cd->ijd", normed, gate_weight, preferred_element_type=f32)
    )
    update = (gate_val * outer_val).astype(bf16)
    upstream = cotangent.astype(f32)
    outer_grad = (upstream * gate_val).astype(bf16)
    gate_grad = (upstream * outer_val * gate_val * (1.0 - gate_val)).astype(bf16)
    tnorm_grad = jnp.einsum("ijc,hc->ijh", outer_grad, out_weight, preferred_element_type=f32)
    hat_grad = tnorm_grad * out_gain
    tri_grad = (
        tri_scale
        * (
            hat_grad
            - jnp.mean(hat_grad, axis=-1, keepdims=True)
            - tri_hat * jnp.mean(hat_grad * tri_hat, axis=-1, keepdims=True)
        )
    ).astype(bf16)
    grad_all = whole(exchange(to_channels(tri_grad.transpose(2, 0, 1))))
    row_own = jnp.einsum("hij,hjk->hik", grad_all, right_all, preferred_element_type=f32)
    col_own = jnp.einsum("hij,hik->hjk", grad_all, left_all, preferred_element_type=f32)
    back = exchange(jnp.stack([tiles(row_own), tiles(col_own)], axis=1))
    row_part = back[:, 0].reshape(hidden, rows_dev, cols_dev).astype(f32)
    col_part = back[:, 1].reshape(hidden, rows_dev, cols_dev).astype(f32)

    def push_back(part, values, sig, weight):
        part = part * mask[None] * sig
        combined = jnp.concatenate([part, part * values * (1.0 - sig)], axis=0).astype(bf16)
        panel_grad = jnp.einsum("hik,ch->ikc", combined, weight, preferred_element_type=f32)
        weight_grad = jnp.einsum("ikc,hik->ch", normed, combined, preferred_element_type=f32)
        return panel_grad, weight_grad

    grad_output = jnp.einsum("ijh,ijc->hc", tri_normed, outer_grad, preferred_element_type=f32)
    grad_gating = jnp.einsum("ijc,ijd->cd", normed, gate_grad, preferred_element_type=f32)
    from_rows, grad_left = push_back(row_part, left_val, left_sig, left_weight)
    from_cols, grad_right = push_back(col_part, right_val, right_sig, right_weight)
    gate_back = jnp.einsum("ijd,cd->ijc", gate_grad, gate_weight, preferred_element_type=f32)
    normed_grad = gate_back + from_rows + from_cols
    scaled = normed_grad * norm_gain
    grad_pair = (
        pair_scale
        * (
            scaled
            - jnp.mean(scaled, axis=-1, keepdims=True)
            - pair_hat * jnp.mean(scaled * pair_hat, axis=-1, keepdims=True)
        )
    ).astype(bf16)
    early = jnp.concatenate(
        [
            grad_gating,
            grad_output,
            jnp.sum(tnorm_grad * tri_hat, axis=(0, 1))[None],
            jnp.sum(tnorm_grad, axis=(0, 1))[None],
        ],
        axis=0,
    )
    late = jnp.concatenate(
        [
            grad_left[:, :hidden],
            grad_left[:, hidden:],
            grad_right[:, :hidden],
            grad_right[:, hidden:],
            jnp.sum(normed_grad * pair_hat, axis=(0, 1))[None],
            jnp.sum(normed_grad, axis=(0, 1))[None],
        ],
        axis=0,
    )
    inverse = 1.0 / tokens
    early = total_sum(early, n_dev) * inverse
    late = total_sum(late, n_dev) * inverse
    c = channels
    return (
        update,
        grad_pair,
        jnp.concatenate([late[:c], late[c : 2 * c]], axis=1),
        jnp.concatenate([late[2 * c : 3 * c], late[3 * c : 4 * c]], axis=1),
        early[:c],
        early[c : c + hidden],
        jnp.concatenate([late[4 * c : 4 * c + 2], early[c + hidden : c + hidden + 2]], axis=0),
    )


def solution(mesh):
    return jax.shard_map(
        per_device,
        mesh=mesh,
        in_specs=(P("row", "col", None), P("row", "col", None)) + (P(),) * 9,
        out_specs=(P("row", "col", None), P("row", "col", None), P(), P(), P(), P(), P()),
        check_vma=False,
    )
```

```python
import functools

import jax
import jax.numpy as jnp
from jax import lax
from jax.experimental import pallas as pl
from jax.experimental.pallas import tpu as pltpu
from jax.sharding import PartitionSpec as P

EPS = 1e-05
BOTH = ("row", "col")
LANES = 128
F32, BF16 = jnp.float32, jnp.bfloat16
NN = (((1,), (0,)), ((), ()))
NT = (((1,), (1,)), ((), ()))
TN = (((0,), (0,)), ((), ()))
VMEM = pl.BlockSpec(memory_space=pltpu.VMEM)
SMEM = pl.BlockSpec(memory_space=pltpu.SMEM)


def dot(a, b, dims=NN):
    return lax.dot_general(a, b, dims, preferred_element_type=F32)


def call(body, outs, scratch, name, flops, moved):
    return pl.pallas_call(
        body,
        out_shape=tuple(jax.ShapeDtypeStruct(s, d) for s, d in outs),
        out_specs=tuple(VMEM for _ in outs),
        scratch_shapes=scratch,
        name=name,
        compiler_params=pltpu.CompilerParams(vmem_limit_bytes=24 * 2**20),
        cost_estimate=pl.CostEstimate(flops=flops, bytes_accessed=moved, transcendentals=0),
    )


def exchange(blocks):
    return lax.all_to_all(blocks, BOTH, split_axis=0, concat_axis=0, tiled=True)


def swap_halves(a, b):
    half = LANES // 2
    first = jnp.concatenate([a[:, :half], b[:, :half]], axis=1)
    second = jnp.concatenate([a[:, half:], b[:, half:]], axis=1)
    return first, second


def column(row):
    return jnp.broadcast_to(row, (LANES, row.shape[1])).T


def flip(weight):
    return weight.astype(F32).T.astype(BF16)


def token_tile(ref, p, half):
    return jnp.concatenate([ref[p], ref[half + p]], axis=0)


def mask_row(info, p, half, cols):
    lane = lax.broadcasted_iota(jnp.int32, (1, LANES), 1)
    second = (lane >= cols).astype(jnp.int32)
    row = info[0] + p + half * second
    col = info[1] + lane - cols * second
    return ((row < info[2]) & (col < info[2])).astype(F32)


def normal(x, axis):
    center = x - jnp.mean(x, axis=axis, keepdims=True)
    inverse = lax.rsqrt(jnp.mean(center * center, axis=axis, keepdims=True) + EPS)
    return center * inverse, inverse


def project(half, hidden, info, pair, gain, bias, lw, rw, send, nt_out, wt, gb, ls, rs):
    n_dev, _, per, _ = send.shape
    cols = pair.shape[1]
    wt[0] = flip(lw[...])
    wt[1] = flip(rw[...])
    gb[0] = column(gain[...])
    gb[1] = column(bias[...])

    def step(p, carry):
        x = token_tile(pair, p, half).astype(F32).T
        hat, _ = normal(x, 0)
        nt = (hat * gb[0] + gb[1]).astype(BF16)
        nt_out[:, pl.ds(pl.multiple_of(p * LANES, LANES), LANES)] = nt
        mask = mask_row(info, p, half, cols)
        for side, scr in ((0, ls), (1, rs)):
            proj = dot(wt[side], nt)
            act = mask * jax.nn.sigmoid(proj[hidden:]) * proj[:hidden]
            scr[pl.ds(p, hidden, stride=half), :] = act
        return carry

    lax.fori_loop(0, half, step, 0, unroll=2)

    def pack(d, carry):
        at = pl.ds(pl.multiple_of(d * per, per), per)
        send[d, 0] = ls[at, :].astype(BF16)
        send[d, 1] = rs[at, :].astype(BF16)
        return carry

    lax.fori_loop(0, n_dev, pack, 0, unroll=4)


def prepare(half, hidden, info, pair, cot, nt_in, lw, rw, gw, gate_out, cot_out, coef, hat_out, scale_out, wt, gwt):
    cols = pair.shape[1]
    wt[0] = flip(lw[...])
    wt[1] = flip(rw[...])
    gwt[...] = flip(gw[...])

    def step(p, carry):
        at = pl.ds(pl.multiple_of(p * LANES, LANES), LANES)
        x = token_tile(pair, p, half).astype(F32).T
        hat, inverse = normal(x, 0)
        hat_out[:, at] = hat
        scale_out[:, at] = jnp.broadcast_to(inverse, (8, LANES))
        cot_out[:, at] = token_tile(cot, p, half).astype(F32).T
        nt = nt_in[:, at]
        gate_out[:, at] = jax.nn.sigmoid(dot(gwt[...], nt))
        mask = mask_row(info, p, half, cols)
        for side in (0, 1):
            proj = dot(wt[side], nt)
            sig = jax.nn.sigmoid(proj[hidden:])
            coef[2 * side, :, at] = mask * sig
            coef[2 * side + 1, :, at] = mask * proj[:hidden] * sig * (1.0 - sig)
        return carry

    lax.fori_loop(0, half, step, 0, unroll=2)


def gather_whole(n_row, n_col, half, read, write):
    for r in range(n_row):
        for m in range(n_col // 2):
            first, second = swap_halves(read(r * n_col + 2 * m), read(r * n_col + 2 * m + 1))
            write(2 * r * half, m * LANES, first)
            write((2 * r + 1) * half, m * LANES, second)


def scatter_tiles(n_row, n_col, half, whole, write):
    for r in range(n_row):
        for m in range(n_col // 2):
            at = slice(m * LANES, (m + 1) * LANES)
            a = whole[2 * r * half : (2 * r + 1) * half, at]
            b = whole[(2 * r + 1) * half : (2 * r + 2) * half, at]
            first, second = swap_halves(a, b)
            write(r * n_col + 2 * m, first)
            write(r * n_col + 2 * m + 1, second)


def multiply(n_row, n_col, half, recv, send, left, right, acc):
    def step(h, carry):
        at = pl.ds(pl.multiple_of(h * half, half), half)
        for side, out in ((0, left), (1, right)):

            def write(row, lane, block, out=out):
                out[h, row : row + half, lane : lane + LANES] = block

            gather_whole(n_row, n_col, half, lambda d, side=side: recv[d, side, at, :], write)
        acc[...] = dot(left[h], right[h], NT)

        def put(d, block):
            send[d, at, :] = block.astype(BF16)

        scatter_tiles(n_row, n_col, half, acc, put)
        return carry

    lax.fori_loop(0, left.shape[0], step, 0)


def multiply_back(n_row, n_col, half, recv, left, right, send, grad, acc):
    def step(h, carry):
        at = pl.ds(pl.multiple_of(h * half, half), half)

        def write(row, lane, block):
            grad[row : row + half, lane : lane + LANES] = block

        gather_whole(n_row, n_col, half, lambda d: recv[d, at, :], write)
        acc[0] = dot(grad[...], right[h], NN)
        acc[1] = dot(grad[...], left[h], TN)
        for side in (0, 1):

            def put(d, block, side=side):
                send[d, side, at, :] = block.astype(BF16)

            scatter_tiles(n_row, n_col, half, acc.at[side], put)
        return carry

    lax.fori_loop(0, left.shape[0], step, 0)


def unpack(recv, scr, side=None):
    n_dev, per = recv.shape[0], recv.shape[-2]

    def step(d, carry):
        at = pl.ds(pl.multiple_of(d * per, per), per)
        block = recv[d] if side is None else recv[d, side]
        scr[at, :] = block.astype(F32)
        return carry

    lax.fori_loop(0, n_dev, step, 0, unroll=4)


def middle(half, hidden, recv, gate_in, cot_in, gain, bias, ow, send, upd, og_out, gg_out, tn_out, sums, scr, owt, gb):
    n_dev, per, _ = send.shape
    unpack(recv, scr)
    owt[...] = flip(ow[...])
    gb[0] = column(gain[...])
    gb[1] = column(bias[...])
    sums[...] = jnp.zeros_like(sums)

    def step(p, carry):
        at = pl.ds(pl.multiple_of(p * LANES, LANES), LANES)
        rows = pl.ds(p, hidden, stride=half)
        hat, scale = normal(scr[rows, :], 0)
        tn = (hat * gb[0] + gb[1]).astype(BF16)
        tn_out[:, at] = tn
        outer = dot(owt[...], tn)
        gate = gate_in[:, at]
        up = cot_in[:, at]
        upd[:, at] = gate * outer
        og = (up * gate).astype(BF16)
        og_out[:, at] = og
        gg_out[:, at] = (up * outer * gate * (1.0 - gate)).astype(BF16)
        tg = dot(ow[...], og)
        sums[0] += tg * hat
        sums[1] += tg
        hg = tg * gb[0]
        back = hg - jnp.mean(hg, axis=0, keepdims=True)
        back = back - hat * jnp.mean(hg * hat, axis=0, keepdims=True)
        scr[rows, :] = scale * back
        return carry

    lax.fori_loop(0, half, step, 0, unroll=2)

    def pack(d, carry):
        at = pl.ds(pl.multiple_of(d * per, per), per)
        send[d] = scr[at, :].astype(BF16)
        return carry

    lax.fori_loop(0, n_dev, pack, 0, unroll=4)


def fold(x):
    return jnp.sum(x.T, axis=0, keepdims=True)


def settle(half, upd, og, gg, tn, nt, sums, update, early, norms):
    def step(p, carry):
        at = pl.ds(pl.multiple_of(p * LANES, LANES), LANES)
        tile = upd[:, at].T.astype(BF16)
        cols = update.shape[1]
        update[p] = tile[:cols]
        update[half + p] = tile[cols:]
        return carry

    lax.fori_loop(0, half, step, 0, unroll=2)
    early[0] = dot(nt[...], gg[...], NT)
    early[1] = dot(tn[...], og[...], NT)
    norms[0:1] = fold(sums[0])
    norms[1:2] = fold(sums[1])


def finish(half, hidden, recv, coef, nt, gg, hat, lw, rw, gw, early, early_norms, parts, ng_out, scr, comb, sums):
    for side in (0, 1):
        unpack(recv, scr.at[side], side)
    sums[...] = jnp.zeros_like(sums)

    def step(p, carry):
        at = pl.ds(pl.multiple_of(p * LANES, LANES), LANES)
        rows = pl.ds(p, hidden, stride=half)
        ng = dot(gw[...], gg[:, at])
        for side, w in ((0, lw), (1, rw)):
            part = scr[side, rows, :]
            both = jnp.concatenate(
                [part * coef[2 * side, :, at], part * coef[2 * side + 1, :, at]], axis=0
            ).astype(BF16)
            comb[side, :, at] = both
            ng = ng + dot(w[...], both)
        ng_out[:, at] = ng
        sums[0] += ng * hat[:, at]
        sums[1] += ng
        return carry

    lax.fori_loop(0, half, step, 0, unroll=2)
    c = nt.shape[0]
    parts[...] = jnp.zeros_like(parts)
    for side in (0, 1):
        grad = dot(nt[...], comb[side], NT)
        parts[2 * side * c : (2 * side + 1) * c] = grad[:, :hidden].astype(BF16)
        parts[(2 * side + 1) * c : (2 * side + 2) * c] = grad[:, hidden:].astype(BF16)
    parts[4 * c : 5 * c] = early[0].astype(BF16)
    parts[5 * c : 5 * c + hidden] = early[1].astype(BF16)
    exact = jnp.concatenate([fold(sums[0]), fold(sums[1]), early_norms[0:2]], axis=0)
    high = exact.astype(BF16)
    low = (exact - high.astype(F32)).astype(BF16)
    base = 5 * c + hidden
    parts[base : base + 8] = jnp.concatenate([high, low], axis=0)


def add_up(scale, holder, device, recv, send):
    n_dev, share, _ = recv.shape
    mine = scale * jnp.sum(recv[...].astype(F32), axis=0)
    exact = mine[0:4] + mine[4:8]
    high = exact.astype(BF16).astype(F32)
    pairs = jnp.concatenate([high, exact - high], axis=0)
    if share > 8:
        pairs = jnp.concatenate([pairs, mine[8:]], axis=0)
    keep = (device[0] == holder).astype(F32)
    result = (keep * pairs + (1.0 - keep) * mine).astype(BF16)
    for d in range(n_dev):
        send[d] = result


def close(half, ng, hat, scale, gain, grad_pair, gb):
    gb[...] = column(gain[...])
    cols = grad_pair.shape[1]

    def step(p, carry):
        at = pl.ds(pl.multiple_of(p * LANES, LANES), LANES)
        q = ng[:, at] * gb[...]
        h = hat[:, at]
        back = q - jnp.mean(q, axis=0, keepdims=True)
        back = back - h * jnp.mean(q * h, axis=0, keepdims=True)
        tile = (scale[0:1, at] * back).T.astype(BF16)
        grad_pair[p] = tile[:cols]
        grad_pair[half + p] = tile[cols:]
        return carry

    lax.fori_loop(0, half, step, 0, unroll=2)


def per_device(
    pair,
    cotangent,
    length,
    norm_gain,
    norm_bias,
    left_weight,
    right_weight,
    gate_weight,
    out_gain,
    out_bias,
    out_weight,
):
    n_row = lax.axis_size("row")
    n_col = lax.axis_size("col")
    n_dev = n_row * n_col
    rows_dev, cols_dev, c = pair.shape
    tokens = rows_dev * n_row
    hidden = out_weight.shape[0]
    own = hidden // n_dev
    half = rows_dev * cols_dev // LANES
    wide = half * LANES
    per = own * half
    assert 2 * cols_dev == LANES and rows_dev == 2 * half and c == LANES and hidden == LANES
    info = jnp.stack(
        [
            lax.axis_index("row").astype(jnp.int32) * rows_dev,
            lax.axis_index("col").astype(jnp.int32) * cols_dev,
            length[0],
        ]
    )
    gain, bias = norm_gain[None], norm_bias[None]
    o_gain, o_bias = out_gain[None], out_bias[None]
    vm = pltpu.VMEM
    sq = (c, LANES)

    send, nt = call(
        functools.partial(project, half, hidden),
        [((n_dev, 2, per, LANES), BF16), ((c, wide), BF16)],
        [vm((2, 2 * hidden, c), BF16), vm((2,) + sq, F32)] + [vm((hidden * half, LANES), F32)] * 2,
        "project", 300 * 10**6, 3 * 2**20,
    )(info, pair, gain, bias, left_weight, right_weight)
    both = exchange(send)
    gate, cot, coef, hat, scale = call(
        functools.partial(prepare, half, hidden),
        [((c, wide), F32), ((c, wide), F32), ((4, hidden, wide), F32), ((c, wide), F32), ((8, wide), F32)],
        [vm((2, 2 * hidden, c), BF16), vm((c, c), BF16)],
        "prepare", 400 * 10**6, 9 * 2**20,
    )(info, pair, cotangent, nt, left_weight, right_weight, gate_weight)
    send, left, right = call(
        functools.partial(multiply, n_row, n_col, half),
        [((n_dev, per, LANES), BF16), ((own, tokens, tokens), BF16), ((own, tokens, tokens), BF16)],
        [vm((tokens, tokens), F32)],
        "multiply", 200 * 10**6, 3 * 2**20,
    )(both)
    tri = exchange(send)
    send, upd, og, gg, tn, sums = call(
        functools.partial(middle, half, hidden),
        [((n_dev, per, LANES), BF16), ((c, wide), F32)] + [((c, wide), BF16)] * 3 + [((2,) + sq, F32)],
        [vm((hidden * half, LANES), F32), vm((c, hidden), BF16), vm((2,) + sq, F32)],
        "middle", 200 * 10**6, 6 * 2**20,
    )(tri, gate, cot, o_gain, o_bias, out_weight)
    grad = exchange(send)
    update, early, early_norms = call(
        functools.partial(settle, half),
        [((rows_dev, cols_dev, c), BF16), ((2,) + sq, F32), ((8, LANES), F32)],
        [],
        "settle", 200 * 10**6, 4 * 2**20,
    )(upd, og, gg, tn, nt, sums)
    (send,) = call(
        functools.partial(multiply_back, n_row, n_col, half),
        [((n_dev, 2, per, LANES), BF16)],
        [vm((tokens, tokens), BF16), vm((2, tokens, tokens), F32)],
        "multiply_back", 300 * 10**6, 3 * 2**20,
    )(grad, left, right)
    back = exchange(send)
    used = 5 * c + hidden + 8
    assert (5 * c + hidden) % 8 == 0
    share = -(-used // (n_dev * 8)) * 8
    while (5 * c + hidden) % share:
        share += 8
    device = (lax.axis_index("row") * n_col + lax.axis_index("col")).astype(jnp.int32)[None]
    parts, ng = call(
        functools.partial(finish, half, hidden),
        [((n_dev * share, LANES), BF16), ((c, wide), F32)],
        [vm((2, hidden * half, LANES), F32), vm((2, 2 * hidden, wide), BF16), vm((2,) + sq, F32)],
        "finish", 500 * 10**6, 10 * 2**20,
    )(back, coef, nt, gg, hat, left_weight, right_weight, gate_weight, early, early_norms)
    (send,) = call(
        functools.partial(add_up, 1.0 / tokens, (5 * c + hidden) // share),
        [((n_dev, share, LANES), BF16)],
        [],
        "add_up", 10**6, 2**19,
    )(device, exchange(parts.reshape(n_dev, share, LANES)))
    totals = exchange(send).reshape(n_dev * share, LANES).astype(F32)
    (grad_pair,) = call(
        functools.partial(close, half),
        [((rows_dev, cols_dev, c), BF16)],
        [vm(sq, F32)],
        "close", 50 * 10**6, 3 * 2**20,
    )(ng, hat, scale, gain)
    base = 5 * c + hidden
    return (
        update,
        grad_pair,
        jnp.concatenate([totals[:c], totals[c : 2 * c]], axis=1),
        jnp.concatenate([totals[2 * c : 3 * c], totals[3 * c : 4 * c]], axis=1),
        totals[4 * c : 5 * c],
        totals[5 * c : base],
        totals[base : base + 4] + totals[base + 4 : base + 8],
    )


def solution(mesh):
    return jax.shard_map(
        per_device,
        mesh=mesh,
        in_specs=(P("row", "col", None), P("row", "col", None)) + (P(),) * 9,
        out_specs=(P("row", "col", None), P("row", "col", None), P(), P(), P(), P(), P()),
        check_vma=False,
    )
```

```python
import functools

import jax
import jax.numpy as jnp
from jax import lax
from jax.experimental import pallas as pl
from jax.experimental.pallas import tpu as pltpu
from jax.sharding import PartitionSpec as P

EPS = 1e-05
BOTH = ("row", "col")
LANES = 128
F32, BF16 = jnp.float32, jnp.bfloat16
NN = (((1,), (0,)), ((), ()))
NT = (((1,), (1,)), ((), ()))
TN = (((0,), (0,)), ((), ()))
VMEM = pl.BlockSpec(memory_space=pltpu.VMEM)
SMEM = pl.BlockSpec(memory_space=pltpu.SMEM)
HBM = pl.BlockSpec(memory_space=pltpu.HBM)
GROUPS = 4


def dot(a, b, dims=NN):
    return lax.dot_general(a, b, dims, preferred_element_type=F32)


def call(body, ins, outs, scratch, name, flops, moved):
    return pl.pallas_call(
        body,
        in_specs=list(ins),
        out_shape=tuple(jax.ShapeDtypeStruct(s, d) for s, d, _ in outs),
        out_specs=tuple(spec for _, _, spec in outs),
        scratch_shapes=scratch,
        name=name,
        compiler_params=pltpu.CompilerParams(vmem_limit_bytes=20 * 2**20),
        cost_estimate=pl.CostEstimate(flops=flops, bytes_accessed=moved, transcendentals=0),
    )


def begin(source, target, sem):
    copy = pltpu.make_async_copy(source, target, sem)
    copy.start()
    return copy


def finish_all(copies):
    for copy in copies:
        copy.wait()


def span(g, size):
    return pl.ds(g * size, size)


def exchange(blocks):
    return lax.all_to_all(blocks, BOTH, split_axis=0, concat_axis=0, tiled=True)


def swap_halves(a, b):
    half = LANES // 2
    first = jnp.concatenate([a[:, :half], b[:, :half]], axis=1)
    second = jnp.concatenate([a[:, half:], b[:, half:]], axis=1)
    return first, second


def column(row):
    return jnp.broadcast_to(row, (LANES, row.shape[1])).T


def flip(weight):
    return weight.astype(F32).T.astype(BF16)


def token_tile(ref, p, half):
    return jnp.concatenate([ref[p], ref[half + p]], axis=0)


def mask_row(length, p, half, cols):
    lane = lax.broadcasted_iota(jnp.int32, (1, LANES), 1)
    second = (lane >= cols).astype(jnp.int32)
    row = lax.axis_index("row") * (2 * half) + p + half * second
    col = lax.axis_index("col") * cols + lane - cols * second
    return ((row < length[0]) & (col < length[0])).astype(F32)


def normal(x, axis):
    center = x - jnp.mean(x, axis=axis, keepdims=True)
    inverse = lax.rsqrt(jnp.mean(center * center, axis=axis, keepdims=True) + EPS)
    return center * inverse, inverse


def project(half, hidden, length, pair_h, gain_h, bias_h, lw_h, rw_h, send, nt_out, pair, gain, bias, w, wt, gb, ls, rs, sems):
    n_dev, _, per, _ = send.shape
    cols = pair.shape[1]
    step_rows = half // GROUPS
    small = [
        begin(lw_h, w.at[0], sems.at[0]),
        begin(rw_h, w.at[1], sems.at[1]),
        begin(gain_h, gain, sems.at[2]),
        begin(bias_h, bias, sems.at[3]),
    ]
    tiles = []
    for g in range(GROUPS):
        for k in (0, 1):
            at = pl.ds(k * half + g * step_rows, step_rows)
            tiles.append(begin(pair_h.at[at], pair.at[at], sems.at[4 + 2 * g + k]))
    finish_all(small)
    wt[0] = flip(w[0])
    wt[1] = flip(w[1])
    gb[0] = column(gain[...])
    gb[1] = column(bias[...])

    def step(p, carry):
        x = token_tile(pair, p, half).astype(F32).T
        hat, _ = normal(x, 0)
        nt = (hat * gb[0] + gb[1]).astype(BF16)
        nt_out[:, pl.ds(pl.multiple_of(p * LANES, LANES), LANES)] = nt
        mask = mask_row(length, p, half, cols)
        for side, scr in ((0, ls), (1, rs)):
            proj = dot(wt[side], nt)
            act = mask * jax.nn.sigmoid(proj[hidden:]) * proj[:hidden]
            scr[pl.ds(p, hidden, stride=half), :] = act
        return carry

    for g in range(GROUPS):
        finish_all(tiles[2 * g : 2 * g + 2])
        lax.fori_loop(g * step_rows, (g + 1) * step_rows, step, 0, unroll=2)

    def pack(d, carry):
        at = pl.ds(pl.multiple_of(d * per, per), per)
        send[d, 0] = ls[at, :].astype(BF16)
        send[d, 1] = rs[at, :].astype(BF16)
        return carry

    lax.fori_loop(0, n_dev, pack, 0, unroll=4)


def prepare(half, hidden, length, pair, cot, nt_in, lw, rw, gw, gate_out, cot_out, coef, hat_out, scale_out, wt, gwt):
    cols = pair.shape[1]
    wt[0] = flip(lw[...])
    wt[1] = flip(rw[...])
    gwt[...] = flip(gw[...])

    def step(p, carry):
        at = pl.ds(pl.multiple_of(p * LANES, LANES), LANES)
        x = token_tile(pair, p, half).astype(F32).T
        hat, inverse = normal(x, 0)
        hat_out[:, at] = hat
        scale_out[:, at] = jnp.broadcast_to(inverse, (8, LANES))
        cot_out[:, at] = token_tile(cot, p, half).astype(F32).T.astype(BF16)
        nt = nt_in[:, at]
        gate_out[:, at] = jax.nn.sigmoid(dot(gwt[...], nt))
        mask = mask_row(length, p, half, cols)
        for side in (0, 1):
            proj = dot(wt[side], nt)
            sig = jax.nn.sigmoid(proj[hidden:])
            coef[2 * side, :, at] = mask * sig
            coef[2 * side + 1, :, at] = mask * proj[:hidden] * sig * (1.0 - sig)
        return carry

    lax.fori_loop(0, half, step, 0, unroll=2)


def gather_whole(n_row, n_col, half, read, write):
    for r in range(n_row):
        for m in range(n_col // 2):
            first, second = swap_halves(read(r * n_col + 2 * m), read(r * n_col + 2 * m + 1))
            write(2 * r * half, m * LANES, first)
            write((2 * r + 1) * half, m * LANES, second)


def scatter_tiles(n_row, n_col, half, whole, write):
    for r in range(n_row):
        for m in range(n_col // 2):
            at = slice(m * LANES, (m + 1) * LANES)
            a = whole[2 * r * half : (2 * r + 1) * half, at]
            b = whole[(2 * r + 1) * half : (2 * r + 2) * half, at]
            first, second = swap_halves(a, b)
            write(r * n_col + 2 * m, first)
            write(r * n_col + 2 * m + 1, second)


def multiply(n_row, n_col, half, recv, send_h, left, right, acc, send, sems):
    def step(h, carry):
        at = pl.ds(pl.multiple_of(h * half, half), half)
        for side, out in ((0, left), (1, right)):

            def write(row, lane, block, out=out):
                out[h, row : row + half, lane : lane + LANES] = block

            gather_whole(n_row, n_col, half, lambda d, side=side: recv[d, side, at, :], write)
        acc[...] = dot(left[h], right[h], NT)

        def put(d, block):
            send[d, at, :] = block.astype(BF16)

        scatter_tiles(n_row, n_col, half, acc, put)
        begin(send.at[:, at], send_h.at[:, at], sems.at[h])
        return carry

    own = left.shape[0]
    lax.fori_loop(0, own, step, 0)
    for h in range(own):
        at = span(h, half)
        pltpu.make_async_copy(send.at[:, at], send_h.at[:, at], sems.at[h]).wait()


def multiply_back(n_row, n_col, half, recv, left, right, send_h, grad, acc, send, sems):
    def step(h, carry):
        at = pl.ds(pl.multiple_of(h * half, half), half)

        def write(row, lane, block):
            grad[row : row + half, lane : lane + LANES] = block

        gather_whole(n_row, n_col, half, lambda d: recv[d, at, :], write)
        acc[0] = dot(grad[...], right[h], NN)
        acc[1] = dot(grad[...], left[h], TN)
        for side in (0, 1):

            def put(d, block, side=side):
                send[d, side, at, :] = block.astype(BF16)

            scatter_tiles(n_row, n_col, half, acc.at[side], put)
        begin(send.at[:, :, at], send_h.at[:, :, at], sems.at[h])
        return carry

    own = left.shape[0]
    lax.fori_loop(0, own, step, 0)
    for h in range(own):
        at = span(h, half)
        pltpu.make_async_copy(send.at[:, :, at], send_h.at[:, :, at], sems.at[h]).wait()


def unpack(recv, scr, side=None):
    n_dev, per = recv.shape[0], recv.shape[-2]

    def step(d, carry):
        at = pl.ds(pl.multiple_of(d * per, per), per)
        block = recv[d] if side is None else recv[d, side]
        scr[at, :] = block.astype(F32)
        return carry

    lax.fori_loop(0, n_dev, step, 0, unroll=4)


def middle(half, hidden, recv, gate_h, cot_h, gain, bias, ow, send, upd_h, og_h, gg_h, tn_h, sums, gate_in, cot_in, upd, og_out, gg_out, tn_out, scr, owt, gb, sems, out_sems):
    n_dev, per, _ = send.shape
    size = gate_in.shape[1] // GROUPS
    fetched = []
    for g in range(GROUPS):
        at = span(g, size)
        fetched.append(begin(gate_h.at[:, at], gate_in.at[:, at], sems.at[2 * g]))
        fetched.append(begin(cot_h.at[:, at], cot_in.at[:, at], sems.at[2 * g + 1]))
    unpack(recv, scr)
    owt[...] = flip(ow[...])
    gb[0] = column(gain[...])
    gb[1] = column(bias[...])
    sums[...] = jnp.zeros_like(sums)

    def step(p, carry):
        at = pl.ds(pl.multiple_of(p * LANES, LANES), LANES)
        rows = pl.ds(p, hidden, stride=half)
        hat, scale = normal(scr[rows, :], 0)
        tn = (hat * gb[0] + gb[1]).astype(BF16)
        tn_out[:, at] = tn
        outer = dot(owt[...], tn)
        gate = gate_in[:, at]
        up = cot_in[:, at].astype(F32)
        upd[:, at] = (gate * outer).astype(BF16)
        og = (up * gate).astype(BF16)
        og_out[:, at] = og
        gg_out[:, at] = (up * outer * gate * (1.0 - gate)).astype(BF16)
        tg = dot(ow[...], og)
        sums[0] += tg * hat
        sums[1] += tg
        hg = tg * gb[0]
        back = hg - jnp.mean(hg, axis=0, keepdims=True)
        back = back - hat * jnp.mean(hg * hat, axis=0, keepdims=True)
        scr[rows, :] = scale * back
        return carry

    stored = []
    saved = ((upd, upd_h), (og_out, og_h), (gg_out, gg_h), (tn_out, tn_h))
    for g in range(GROUPS):
        finish_all(fetched[2 * g : 2 * g + 2])
        count = half // GROUPS
        lax.fori_loop(g * count, (g + 1) * count, step, 0, unroll=2)
        at = span(g, size)
        for k, (source, target) in enumerate(saved):
            stored.append(begin(source.at[:, at], target.at[:, at], out_sems.at[4 * g + k]))

    def pack(d, carry):
        at = pl.ds(pl.multiple_of(d * per, per), per)
        send[d] = scr[at, :].astype(BF16)
        return carry

    lax.fori_loop(0, n_dev, pack, 0, unroll=4)
    finish_all(stored)


def fold(x):
    return jnp.sum(x.T, axis=0, keepdims=True)


def settle(half, upd, og, gg, tn, nt, sums, update, early, norms):
    def step(p, carry):
        at = pl.ds(pl.multiple_of(p * LANES, LANES), LANES)
        tile = upd[:, at].astype(F32).T.astype(BF16)
        cols = update.shape[1]
        update[p] = tile[:cols]
        update[half + p] = tile[cols:]
        return carry

    lax.fori_loop(0, half, step, 0, unroll=2)
    early[0] = dot(nt[...], gg[...], NT)
    early[1] = dot(tn[...], og[...], NT)
    norms[0:1] = fold(sums[0])
    norms[1:2] = fold(sums[1])


def finish(half, hidden, recv, coef_h, nt, gg_h, hat_h, lw, rw, gw, early, early_norms, parts, ng_h, coef, gg, hat, ng_out, scr, comb, sums, sems, out_sems):
    size = hat.shape[1] // GROUPS
    fetched = []
    for g in range(GROUPS):
        at = span(g, size)
        fetched.append(begin(coef_h.at[:, :, at], coef.at[:, :, at], sems.at[3 * g]))
        fetched.append(begin(gg_h.at[:, at], gg.at[:, at], sems.at[3 * g + 1]))
        fetched.append(begin(hat_h.at[:, at], hat.at[:, at], sems.at[3 * g + 2]))
    for side in (0, 1):
        unpack(recv, scr.at[side], side)
    sums[...] = jnp.zeros_like(sums)

    def step(p, carry):
        at = pl.ds(pl.multiple_of(p * LANES, LANES), LANES)
        rows = pl.ds(p, hidden, stride=half)
        ng = dot(gw[...], gg[:, at])
        for side, w in ((0, lw), (1, rw)):
            part = scr[side, rows, :]
            both = jnp.concatenate(
                [part * coef[2 * side, :, at], part * coef[2 * side + 1, :, at]], axis=0
            ).astype(BF16)
            comb[side, :, at] = both
            ng = ng + dot(w[...], both)
        ng_out[:, at] = ng
        sums[0] += ng * hat[:, at]
        sums[1] += ng
        return carry

    stored = []
    for g in range(GROUPS):
        finish_all(fetched[3 * g : 3 * g + 3])
        count = half // GROUPS
        lax.fori_loop(g * count, (g + 1) * count, step, 0, unroll=2)
        at = span(g, size)
        stored.append(begin(ng_out.at[:, at], ng_h.at[:, at], out_sems.at[g]))
    c = nt.shape[0]
    parts[...] = jnp.zeros_like(parts)
    for side in (0, 1):
        grad = dot(nt[...], comb[side], NT)
        parts[2 * side * c : (2 * side + 1) * c] = grad[:, :hidden].astype(BF16)
        parts[(2 * side + 1) * c : (2 * side + 2) * c] = grad[:, hidden:].astype(BF16)
    parts[4 * c : 5 * c] = early[0].astype(BF16)
    parts[5 * c : 5 * c + hidden] = early[1].astype(BF16)
    exact = jnp.concatenate([fold(sums[0]), fold(sums[1]), early_norms[0:2]], axis=0)
    high = exact.astype(BF16)
    low = (exact - high.astype(F32)).astype(BF16)
    base = 5 * c + hidden
    parts[base : base + 8] = jnp.concatenate([high, low], axis=0)
    finish_all(stored)


def add_up(scale, holder, n_col, recv, send):
    n_dev, share, _ = recv.shape
    mine = scale * jnp.sum(recv[...].astype(F32), axis=0)
    exact = mine[0:4] + mine[4:8]
    high = exact.astype(BF16).astype(F32)
    pairs = jnp.concatenate([high, exact - high], axis=0)
    if share > 8:
        pairs = jnp.concatenate([pairs, mine[8:]], axis=0)
    keep = (lax.axis_index("row") * n_col + lax.axis_index("col") == holder).astype(F32)
    result = (keep * pairs + (1.0 - keep) * mine).astype(BF16)
    for d in range(n_dev):
        send[d] = result


def deliver(totals, left, right, gating, output, norms):
    c = left.shape[0]

    def rows(k, n=c):
        return totals[k * c : k * c + n].astype(F32)

    for k, out in ((0, left), (2, right)):
        out[:, :LANES] = rows(k)
        out[:, LANES:] = rows(k + 1)
    gating[...] = rows(4)
    output[...] = rows(5)
    exact = rows(6, 8)
    norms[...] = exact[0:4] + exact[4:8]


def close(half, ng, hat, scale, gain, grad_pair, gb):
    gb[...] = column(gain[...])
    cols = grad_pair.shape[1]

    def step(p, carry):
        at = pl.ds(pl.multiple_of(p * LANES, LANES), LANES)
        q = ng[:, at] * gb[...]
        h = hat[:, at]
        back = q - jnp.mean(q, axis=0, keepdims=True)
        back = back - h * jnp.mean(q * h, axis=0, keepdims=True)
        tile = (scale[0:1, at] * back).T.astype(BF16)
        grad_pair[p] = tile[:cols]
        grad_pair[half + p] = tile[cols:]
        return carry

    lax.fori_loop(0, half, step, 0, unroll=2)


def per_device(
    pair,
    cotangent,
    length,
    norm_gain,
    norm_bias,
    left_weight,
    right_weight,
    gate_weight,
    out_gain,
    out_bias,
    out_weight,
):
    n_row = lax.axis_size("row")
    n_col = lax.axis_size("col")
    n_dev = n_row * n_col
    rows_dev, cols_dev, c = pair.shape
    tokens = rows_dev * n_row
    hidden = out_weight.shape[0]
    own = hidden // n_dev
    half = rows_dev * cols_dev // LANES
    wide = half * LANES
    per = own * half
    assert 2 * cols_dev == LANES and rows_dev == 2 * half and c == LANES and hidden == LANES
    gain, bias = norm_gain[None], norm_bias[None]
    o_gain, o_bias = out_gain[None], out_bias[None]
    vm, dma = pltpu.VMEM, pltpu.SemaphoreType.DMA
    sq = (c, LANES)
    rows = hidden * half

    send, nt = call(
        functools.partial(project, half, hidden),
        (SMEM,) + (HBM,) * 5,
        [((n_dev, 2, per, LANES), BF16, VMEM), ((c, wide), BF16, VMEM)],
        [vm(pair.shape, BF16), vm((1, c), F32), vm((1, c), F32), vm((2, c, 2 * hidden), BF16)]
        + [vm((2, 2 * hidden, c), BF16), vm((2,) + sq, F32), vm((rows, LANES), F32)]
        + [vm((rows, LANES), F32), dma((4 + 2 * GROUPS,))],
        "project", 300 * 10**6, 3 * 2**20,
    )(length, pair, gain, bias, left_weight, right_weight)
    both = exchange(send)
    gate, cot, coef, hat, scale = call(
        functools.partial(prepare, half, hidden),
        (SMEM,) + (VMEM,) * 6,
        [((c, wide), F32, VMEM), ((c, wide), BF16, VMEM), ((4, hidden, wide), F32, VMEM)]
        + [((c, wide), F32, VMEM), ((8, wide), F32, VMEM)],
        [vm((2, 2 * hidden, c), BF16), vm((c, c), BF16)],
        "prepare", 400 * 10**6, 9 * 2**20,
    )(length, pair, cotangent, nt, left_weight, right_weight, gate_weight)
    send, left, right = call(
        functools.partial(multiply, n_row, n_col, half),
        (VMEM,),
        [((n_dev, per, LANES), BF16, HBM)] + [((own, tokens, tokens), BF16, VMEM)] * 2,
        [vm((tokens, tokens), F32), vm((n_dev, per, LANES), BF16), dma((own,))],
        "multiply", 200 * 10**6, 3 * 2**20,
    )(both)
    tri = exchange(send)
    send, upd, og, gg, tn, sums = call(
        functools.partial(middle, half, hidden),
        (VMEM, HBM, HBM, VMEM, VMEM, VMEM),
        [((n_dev, per, LANES), BF16, VMEM)] + [((c, wide), BF16, HBM)] * 4 + [((2,) + sq, F32, VMEM)],
        [vm((c, wide), F32)] + [vm((c, wide), BF16)] * 5 + [vm((rows, LANES), F32)]
        + [vm((c, hidden), BF16), vm((2,) + sq, F32), dma((2 * GROUPS,)), dma((4 * GROUPS,))],
        "middle", 200 * 10**6, 6 * 2**20,
    )(tri, gate, cot, o_gain, o_bias, out_weight)
    grad = exchange(send)
    update, early, early_norms = call(
        functools.partial(settle, half),
        (VMEM,) * 6,
        [((rows_dev, cols_dev, c), BF16, VMEM), ((2,) + sq, F32, VMEM), ((8, LANES), F32, VMEM)],
        [],
        "settle", 200 * 10**6, 4 * 2**20,
    )(upd, og, gg, tn, nt, sums)
    (send,) = call(
        functools.partial(multiply_back, n_row, n_col, half),
        (VMEM,) * 3,
        [((n_dev, 2, per, LANES), BF16, HBM)],
        [vm((tokens, tokens), BF16), vm((2, tokens, tokens), F32)]
        + [vm((n_dev, 2, per, LANES), BF16), dma((own,))],
        "multiply_back", 300 * 10**6, 3 * 2**20,
    )(grad, left, right)
    back = exchange(send)
    base = 5 * c + hidden
    assert base % 8 == 0
    share = -(-(base + 8) // (n_dev * 8)) * 8
    while base % share:
        share += 8
    parts, ng = call(
        functools.partial(finish, half, hidden),
        (VMEM, HBM, VMEM, HBM, HBM) + (VMEM,) * 5,
        [((n_dev * share, LANES), BF16, VMEM), ((c, wide), F32, HBM)],
        [vm((4, hidden, wide), F32), vm((c, wide), BF16), vm((c, wide), F32), vm((c, wide), F32)]
        + [vm((2, rows, LANES), F32), vm((2, 2 * hidden, wide), BF16), vm((2,) + sq, F32)]
        + [dma((3 * GROUPS,)), dma((GROUPS,))],
        "finish", 500 * 10**6, 10 * 2**20,
    )(back, coef, nt, gg, hat, left_weight, right_weight, gate_weight, early, early_norms)
    (send,) = call(
        functools.partial(add_up, 1.0 / tokens, base // share, n_col),
        (VMEM,),
        [((n_dev, share, LANES), BF16, VMEM)],
        [],
        "add_up", 10**6, 2**19,
    )(exchange(parts.reshape(n_dev, share, LANES)))
    totals = exchange(send).reshape(n_dev * share, LANES)
    (grad_pair,) = call(
        functools.partial(close, half),
        (VMEM,) * 4,
        [((rows_dev, cols_dev, c), BF16, VMEM)],
        [vm(sq, F32)],
        "close", 50 * 10**6, 3 * 2**20,
    )(ng, hat, scale, gain)
    grads = call(
        deliver,
        (VMEM,),
        [((c, 2 * hidden), F32, VMEM)] * 2
        + [((c, c), F32, VMEM), ((hidden, c), F32, VMEM), ((4, c), F32, VMEM)],
        [],
        "deliver", 10**6, 2**20,
    )(totals)
    return (update, grad_pair) + tuple(grads)


def solution(mesh):
    return jax.shard_map(
        per_device,
        mesh=mesh,
        in_specs=(P("row", "col", None), P("row", "col", None)) + (P(),) * 9,
        out_specs=(P("row", "col", None), P("row", "col", None), P(), P(), P(), P(), P()),
        check_vma=False,
    )
```

```python
import functools

import jax
import jax.numpy as jnp
from jax import lax
from jax.experimental import pallas as pl
from jax.experimental.pallas import tpu as pltpu
from jax.sharding import PartitionSpec as P

EPS = 1e-05
BOTH = ("row", "col")
LANES = 128
F32, BF16 = jnp.float32, jnp.bfloat16
NN = (((1,), (0,)), ((), ()))
NT = (((1,), (1,)), ((), ()))
TN = (((0,), (0,)), ((), ()))
VMEM = pl.BlockSpec(memory_space=pltpu.VMEM)
SMEM = pl.BlockSpec(memory_space=pltpu.SMEM)
HBM = pl.BlockSpec(memory_space=pltpu.HBM)
GROUPS = 4


def dot(a, b, dims=NN):
    return lax.dot_general(a, b, dims, preferred_element_type=F32)


def call(body, ins, outs, scratch, name, flops, moved):
    run = pl.pallas_call(
        body,
        in_specs=list(ins),
        out_shape=tuple(
            pltpu.HBM(s, d) if spec is HBM else jax.ShapeDtypeStruct(s, d) for s, d, spec in outs
        ),
        out_specs=tuple(spec for _, _, spec in outs),
        scratch_shapes=scratch,
        name=name,
        compiler_params=pltpu.CompilerParams(vmem_limit_bytes=20 * 2**20),
        cost_estimate=pl.CostEstimate(flops=flops, bytes_accessed=moved, transcendentals=0),
    )

    def placed(*args):
        return run(
            *[
                pltpu.with_memory_space_constraint(x, pltpu.HBM) if spec is HBM else x
                for x, spec in zip(args, ins, strict=True)
            ]
        )

    return placed


def begin(source, target, sem):
    copy = pltpu.make_async_copy(source, target, sem)
    copy.start()
    return copy


def finish_all(copies):
    for copy in copies:
        copy.wait()


def span(g, size):
    return pl.ds(g * size, size)


def exchange(blocks):
    return lax.all_to_all(blocks, BOTH, split_axis=0, concat_axis=0, tiled=True)


def swap_halves(a, b):
    half = LANES // 2
    first = jnp.concatenate([a[:, :half], b[:, :half]], axis=1)
    second = jnp.concatenate([a[:, half:], b[:, half:]], axis=1)
    return first, second


def column(row):
    return jnp.broadcast_to(row, (LANES, row.shape[1])).T


def flip(weight):
    return weight.astype(F32).T.astype(BF16)


def token_tile(ref, p, half):
    return jnp.concatenate([ref[p], ref[half + p]], axis=0)


def mask_row(length, p, half, cols):
    lane = lax.broadcasted_iota(jnp.int32, (1, LANES), 1)
    second = (lane >= cols).astype(jnp.int32)
    row = lax.axis_index("row") * (2 * half) + p + half * second
    col = lax.axis_index("col") * cols + lane - cols * second
    return ((row < length[0]) & (col < length[0])).astype(F32)


def normal(x, axis):
    center = x - jnp.mean(x, axis=axis, keepdims=True)
    inverse = lax.rsqrt(jnp.mean(center * center, axis=axis, keepdims=True) + EPS)
    return center * inverse, inverse


def project(half, hidden, length, pair_h, gain_h, bias_h, lw_h, rw_h, send, nt_out, pair, gain, bias, w, wt, gb, ls, rs, sems):
    n_dev, _, per, _ = send.shape
    cols = pair.shape[1]
    step_rows = half // GROUPS
    small = [
        begin(lw_h, w.at[0], sems.at[0]),
        begin(rw_h, w.at[1], sems.at[1]),
        begin(gain_h, gain, sems.at[2]),
        begin(bias_h, bias, sems.at[3]),
    ]
    tiles = []
    for g in range(GROUPS):
        for k in (0, 1):
            at = pl.ds(k * half + g * step_rows, step_rows)
            tiles.append(begin(pair_h.at[at], pair.at[at], sems.at[4 + 2 * g + k]))
    finish_all(small)
    wt[0] = flip(w[0])
    wt[1] = flip(w[1])
    gb[0] = column(gain[...])
    gb[1] = column(bias[...])

    def step(p, carry):
        x = token_tile(pair, p, half).astype(F32).T
        hat, _ = normal(x, 0)
        nt = (hat * gb[0] + gb[1]).astype(BF16)
        nt_out[:, pl.ds(pl.multiple_of(p * LANES, LANES), LANES)] = nt
        mask = mask_row(length, p, half, cols)
        for side, scr in ((0, ls), (1, rs)):
            proj = dot(wt[side], nt)
            act = mask * jax.nn.sigmoid(proj[hidden:]) * proj[:hidden]
            scr[pl.ds(p, hidden, stride=half), :] = act
        return carry

    for g in range(GROUPS):
        finish_all(tiles[2 * g : 2 * g + 2])
        lax.fori_loop(g * step_rows, (g + 1) * step_rows, step, 0, unroll=2)

    def pack(d, carry):
        at = pl.ds(pl.multiple_of(d * per, per), per)
        send[d, 0] = ls[at, :].astype(BF16)
        send[d, 1] = rs[at, :].astype(BF16)
        return carry

    lax.fori_loop(0, n_dev, pack, 0, unroll=4)


def prepare(half, hidden, length, pair, cot, nt_in, lw, rw, gw, gate_out, cot_out, coef, hat_out, scale_out, wt, gwt):
    cols = pair.shape[1]
    wt[0] = flip(lw[...])
    wt[1] = flip(rw[...])
    gwt[...] = flip(gw[...])

    def step(p, carry):
        at = pl.ds(pl.multiple_of(p * LANES, LANES), LANES)
        x = token_tile(pair, p, half).astype(F32).T
        hat, inverse = normal(x, 0)
        hat_out[:, at] = hat
        scale_out[:, at] = jnp.broadcast_to(inverse, (8, LANES))
        cot_out[:, at] = token_tile(cot, p, half).astype(F32).T.astype(BF16)
        nt = nt_in[:, at]
        gate_out[:, at] = jax.nn.sigmoid(dot(gwt[...], nt))
        mask = mask_row(length, p, half, cols)
        for side in (0, 1):
            proj = dot(wt[side], nt)
            sig = jax.nn.sigmoid(proj[hidden:])
            coef[2 * side, :, at] = mask * sig
            coef[2 * side + 1, :, at] = mask * proj[:hidden] * sig * (1.0 - sig)
        return carry

    lax.fori_loop(0, half, step, 0, unroll=2)


def gather_whole(n_row, n_col, half, read, write):
    for r in range(n_row):
        for m in range(n_col // 2):
            first, second = swap_halves(read(r * n_col + 2 * m), read(r * n_col + 2 * m + 1))
            write(2 * r * half, m * LANES, first)
            write((2 * r + 1) * half, m * LANES, second)


def scatter_tiles(n_row, n_col, half, whole, write):
    for r in range(n_row):
        for m in range(n_col // 2):
            at = slice(m * LANES, (m + 1) * LANES)
            a = whole[2 * r * half : (2 * r + 1) * half, at]
            b = whole[(2 * r + 1) * half : (2 * r + 2) * half, at]
            first, second = swap_halves(a, b)
            write(r * n_col + 2 * m, first)
            write(r * n_col + 2 * m + 1, second)


def multiply(n_row, n_col, half, recv, send_h, left, right, acc, send, sems):
    def step(h, carry):
        at = pl.ds(pl.multiple_of(h * half, half), half)
        for side, out in ((0, left), (1, right)):

            def write(row, lane, block, out=out):
                out[h, row : row + half, lane : lane + LANES] = block

            gather_whole(n_row, n_col, half, lambda d, side=side: recv[d, side, at, :], write)
        acc[...] = dot(left[h], right[h], NT)

        def put(d, block):
            send[d, at, :] = block.astype(BF16)

        scatter_tiles(n_row, n_col, half, acc, put)
        begin(send.at[:, at], send_h.at[:, at], sems.at[h])
        return carry

    own = left.shape[0]
    lax.fori_loop(0, own, step, 0)
    for h in range(own):
        at = span(h, half)
        pltpu.make_async_copy(send.at[:, at], send_h.at[:, at], sems.at[h]).wait()


def multiply_back(n_row, n_col, half, recv, left, right, send_h, grad, acc, send, sems):
    def step(h, carry):
        at = pl.ds(pl.multiple_of(h * half, half), half)

        def write(row, lane, block):
            grad[row : row + half, lane : lane + LANES] = block

        gather_whole(n_row, n_col, half, lambda d: recv[d, at, :], write)
        acc[0] = dot(grad[...], right[h], NN)
        acc[1] = dot(grad[...], left[h], TN)
        for side in (0, 1):

            def put(d, block, side=side):
                send[d, side, at, :] = block.astype(BF16)

            scatter_tiles(n_row, n_col, half, acc.at[side], put)
        begin(send.at[:, :, at], send_h.at[:, :, at], sems.at[h])
        return carry

    own = left.shape[0]
    lax.fori_loop(0, own, step, 0)
    for h in range(own):
        at = span(h, half)
        pltpu.make_async_copy(send.at[:, :, at], send_h.at[:, :, at], sems.at[h]).wait()


def unpack(recv, scr, side=None):
    n_dev, per = recv.shape[0], recv.shape[-2]

    def step(d, carry):
        at = pl.ds(pl.multiple_of(d * per, per), per)
        block = recv[d] if side is None else recv[d, side]
        scr[at, :] = block.astype(F32)
        return carry

    lax.fori_loop(0, n_dev, step, 0, unroll=4)


def middle(half, hidden, recv, gate_h, cot_h, gain, bias, ow, send, upd_h, og_h, gg_h, tn_h, sums, gate_in, cot_in, upd, og_out, gg_out, tn_out, scr, owt, gb, sems, out_sems):
    n_dev, per, _ = send.shape
    size = gate_in.shape[1] // GROUPS
    fetched = []
    for g in range(GROUPS):
        at = span(g, size)
        fetched.append(begin(gate_h.at[:, at], gate_in.at[:, at], sems.at[2 * g]))
        fetched.append(begin(cot_h.at[:, at], cot_in.at[:, at], sems.at[2 * g + 1]))
    unpack(recv, scr)
    owt[...] = flip(ow[...])
    gb[0] = column(gain[...])
    gb[1] = column(bias[...])
    sums[...] = jnp.zeros_like(sums)

    def step(p, carry):
        at = pl.ds(pl.multiple_of(p * LANES, LANES), LANES)
        rows = pl.ds(p, hidden, stride=half)
        hat, scale = normal(scr[rows, :], 0)
        tn = (hat * gb[0] + gb[1]).astype(BF16)
        tn_out[:, at] = tn
        outer = dot(owt[...], tn)
        gate = gate_in[:, at]
        up = cot_in[:, at].astype(F32)
        upd[:, at] = (gate * outer).astype(BF16)
        og = (up * gate).astype(BF16)
        og_out[:, at] = og
        gg_out[:, at] = (up * outer * gate * (1.0 - gate)).astype(BF16)
        tg = dot(ow[...], og)
        sums[0] += tg * hat
        sums[1] += tg
        hg = tg * gb[0]
        back = hg - jnp.mean(hg, axis=0, keepdims=True)
        back = back - hat * jnp.mean(hg * hat, axis=0, keepdims=True)
        scr[rows, :] = scale * back
        return carry

    stored = []
    saved = ((upd, upd_h), (og_out, og_h), (gg_out, gg_h), (tn_out, tn_h))
    for g in range(GROUPS):
        finish_all(fetched[2 * g : 2 * g + 2])
        count = half // GROUPS
        lax.fori_loop(g * count, (g + 1) * count, step, 0, unroll=2)
        at = span(g, size)
        for k, (source, target) in enumerate(saved):
            stored.append(begin(source.at[:, at], target.at[:, at], out_sems.at[4 * g + k]))

    def pack(d, carry):
        at = pl.ds(pl.multiple_of(d * per, per), per)
        send[d] = scr[at, :].astype(BF16)
        return carry

    lax.fori_loop(0, n_dev, pack, 0, unroll=4)
    finish_all(stored)


def fold(x):
    return jnp.sum(x.T, axis=0, keepdims=True)


def settle(half, upd, og, gg, tn, nt, sums, update, early, norms):
    def step(p, carry):
        at = pl.ds(pl.multiple_of(p * LANES, LANES), LANES)
        tile = upd[:, at].astype(F32).T.astype(BF16)
        cols = update.shape[1]
        update[p] = tile[:cols]
        update[half + p] = tile[cols:]
        return carry

    lax.fori_loop(0, half, step, 0, unroll=2)
    early[0] = dot(nt[...], gg[...], NT)
    early[1] = dot(tn[...], og[...], NT)
    norms[0:1] = fold(sums[0])
    norms[1:2] = fold(sums[1])


def finish(half, hidden, recv, coef_h, nt, gg_h, hat_h, lw, rw, gw, early, early_norms, parts, ng_h, coef, gg, hat, ng_out, scr, comb, sums, sems, out_sems):
    size = hat.shape[1] // GROUPS
    fetched = []
    for g in range(GROUPS):
        at = span(g, size)
        fetched.append(begin(coef_h.at[:, :, at], coef.at[:, :, at], sems.at[3 * g]))
        fetched.append(begin(gg_h.at[:, at], gg.at[:, at], sems.at[3 * g + 1]))
        fetched.append(begin(hat_h.at[:, at], hat.at[:, at], sems.at[3 * g + 2]))
    for side in (0, 1):
        unpack(recv, scr.at[side], side)
    sums[...] = jnp.zeros_like(sums)

    def step(p, carry):
        at = pl.ds(pl.multiple_of(p * LANES, LANES), LANES)
        rows = pl.ds(p, hidden, stride=half)
        ng = dot(gw[...], gg[:, at])
        for side, w in ((0, lw), (1, rw)):
            part = scr[side, rows, :]
            both = jnp.concatenate(
                [part * coef[2 * side, :, at], part * coef[2 * side + 1, :, at]], axis=0
            ).astype(BF16)
            comb[side, :, at] = both
            ng = ng + dot(w[...], both)
        ng_out[:, at] = ng
        sums[0] += ng * hat[:, at]
        sums[1] += ng
        return carry

    stored = []
    for g in range(GROUPS):
        finish_all(fetched[3 * g : 3 * g + 3])
        count = half // GROUPS
        lax.fori_loop(g * count, (g + 1) * count, step, 0, unroll=2)
        at = span(g, size)
        stored.append(begin(ng_out.at[:, at], ng_h.at[:, at], out_sems.at[g]))
    c = nt.shape[0]
    parts[...] = jnp.zeros_like(parts)
    for side in (0, 1):
        grad = dot(nt[...], comb[side], NT)
        parts[2 * side * c : (2 * side + 1) * c] = grad[:, :hidden].astype(BF16)
        parts[(2 * side + 1) * c : (2 * side + 2) * c] = grad[:, hidden:].astype(BF16)
    parts[4 * c : 5 * c] = early[0].astype(BF16)
    parts[5 * c : 5 * c + hidden] = early[1].astype(BF16)
    exact = jnp.concatenate([fold(sums[0]), fold(sums[1]), early_norms[0:2]], axis=0)
    high = exact.astype(BF16)
    low = (exact - high.astype(F32)).astype(BF16)
    base = 5 * c + hidden
    parts[base : base + 8] = jnp.concatenate([high, low], axis=0)
    finish_all(stored)


def add_up(scale, holder, n_col, recv, send):
    n_dev, share, _ = recv.shape
    mine = scale * jnp.sum(recv[...].astype(F32), axis=0)
    exact = mine[0:4] + mine[4:8]
    high = exact.astype(BF16).astype(F32)
    pairs = jnp.concatenate([high, exact - high], axis=0)
    if share > 8:
        pairs = jnp.concatenate([pairs, mine[8:]], axis=0)
    keep = (lax.axis_index("row") * n_col + lax.axis_index("col") == holder).astype(F32)
    result = (keep * pairs + (1.0 - keep) * mine).astype(BF16)
    for d in range(n_dev):
        send[d] = result


def deliver(totals, left, right, gating, output, norms):
    c = left.shape[0]

    def rows(k, n=c):
        return totals[k * c : k * c + n].astype(F32)

    for k, out in ((0, left), (2, right)):
        out[:, :LANES] = rows(k)
        out[:, LANES:] = rows(k + 1)
    gating[...] = rows(4)
    output[...] = rows(5)
    exact = rows(6, 8)
    norms[...] = exact[0:4] + exact[4:8]


def close(half, ng, hat, scale, gain, grad_pair, gb):
    gb[...] = column(gain[...])
    cols = grad_pair.shape[1]

    def step(p, carry):
        at = pl.ds(pl.multiple_of(p * LANES, LANES), LANES)
        q = ng[:, at] * gb[...]
        h = hat[:, at]
        back = q - jnp.mean(q, axis=0, keepdims=True)
        back = back - h * jnp.mean(q * h, axis=0, keepdims=True)
        tile = (scale[0:1, at] * back).T.astype(BF16)
        grad_pair[p] = tile[:cols]
        grad_pair[half + p] = tile[cols:]
        return carry

    lax.fori_loop(0, half, step, 0, unroll=2)


def per_device(
    pair,
    cotangent,
    length,
    norm_gain,
    norm_bias,
    left_weight,
    right_weight,
    gate_weight,
    out_gain,
    out_bias,
    out_weight,
):
    n_row = lax.axis_size("row")
    n_col = lax.axis_size("col")
    n_dev = n_row * n_col
    rows_dev, cols_dev, c = pair.shape
    tokens = rows_dev * n_row
    hidden = out_weight.shape[0]
    own = hidden // n_dev
    half = rows_dev * cols_dev // LANES
    wide = half * LANES
    per = own * half
    assert 2 * cols_dev == LANES and rows_dev == 2 * half and c == LANES and hidden == LANES
    gain, bias = norm_gain[None], norm_bias[None]
    o_gain, o_bias = out_gain[None], out_bias[None]
    vm, dma = pltpu.VMEM, pltpu.SemaphoreType.DMA
    sq = (c, LANES)
    rows = hidden * half

    send, nt = call(
        functools.partial(project, half, hidden),
        (SMEM,) + (HBM,) * 5,
        [((n_dev, 2, per, LANES), BF16, VMEM), ((c, wide), BF16, VMEM)],
        [vm(pair.shape, BF16), vm((1, c), F32), vm((1, c), F32), vm((2, c, 2 * hidden), BF16)]
        + [vm((2, 2 * hidden, c), BF16), vm((2,) + sq, F32), vm((rows, LANES), F32)]
        + [vm((rows, LANES), F32), dma((4 + 2 * GROUPS,))],
        "project", 300 * 10**6, 3 * 2**20,
    )(length, pair, gain, bias, left_weight, right_weight)
    both = exchange(send)
    gate, cot, coef, hat, scale = call(
        functools.partial(prepare, half, hidden),
        (SMEM,) + (VMEM,) * 6,
        [((c, wide), F32, VMEM), ((c, wide), BF16, VMEM), ((4, hidden, wide), F32, VMEM)]
        + [((c, wide), F32, VMEM), ((8, wide), F32, VMEM)],
        [vm((2, 2 * hidden, c), BF16), vm((c, c), BF16)],
        "prepare", 400 * 10**6, 9 * 2**20,
    )(length, pair, cotangent, nt, left_weight, right_weight, gate_weight)
    send, left, right = call(
        functools.partial(multiply, n_row, n_col, half),
        (VMEM,),
        [((n_dev, per, LANES), BF16, HBM)] + [((own, tokens, tokens), BF16, VMEM)] * 2,
        [vm((tokens, tokens), F32), vm((n_dev, per, LANES), BF16), dma((own,))],
        "multiply", 200 * 10**6, 3 * 2**20,
    )(both)
    tri = exchange(send)
    send, upd, og, gg, tn, sums = call(
        functools.partial(middle, half, hidden),
        (VMEM, HBM, HBM, VMEM, VMEM, VMEM),
        [((n_dev, per, LANES), BF16, VMEM)] + [((c, wide), BF16, HBM)] * 4 + [((2,) + sq, F32, VMEM)],
        [vm((c, wide), F32)] + [vm((c, wide), BF16)] * 5 + [vm((rows, LANES), F32)]
        + [vm((c, hidden), BF16), vm((2,) + sq, F32), dma((2 * GROUPS,)), dma((4 * GROUPS,))],
        "middle", 200 * 10**6, 6 * 2**20,
    )(tri, gate, cot, o_gain, o_bias, out_weight)
    grad = exchange(send)
    update, early, early_norms = call(
        functools.partial(settle, half),
        (VMEM,) * 6,
        [((rows_dev, cols_dev, c), BF16, VMEM), ((2,) + sq, F32, VMEM), ((8, LANES), F32, VMEM)],
        [],
        "settle", 200 * 10**6, 4 * 2**20,
    )(upd, og, gg, tn, nt, sums)
    (send,) = call(
        functools.partial(multiply_back, n_row, n_col, half),
        (VMEM,) * 3,
        [((n_dev, 2, per, LANES), BF16, HBM)],
        [vm((tokens, tokens), BF16), vm((2, tokens, tokens), F32)]
        + [vm((n_dev, 2, per, LANES), BF16), dma((own,))],
        "multiply_back", 300 * 10**6, 3 * 2**20,
    )(grad, left, right)
    back = exchange(send)
    base = 5 * c + hidden
    assert base % 8 == 0
    share = -(-(base + 8) // (n_dev * 8)) * 8
    while base % share:
        share += 8
    parts, ng = call(
        functools.partial(finish, half, hidden),
        (VMEM, HBM, VMEM, HBM, HBM) + (VMEM,) * 5,
        [((n_dev * share, LANES), BF16, VMEM), ((c, wide), F32, HBM)],
        [vm((4, hidden, wide), F32), vm((c, wide), BF16), vm((c, wide), F32), vm((c, wide), F32)]
        + [vm((2, rows, LANES), F32), vm((2, 2 * hidden, wide), BF16), vm((2,) + sq, F32)]
        + [dma((3 * GROUPS,)), dma((GROUPS,))],
        "finish", 500 * 10**6, 10 * 2**20,
    )(back, coef, nt, gg, hat, left_weight, right_weight, gate_weight, early, early_norms)
    (send,) = call(
        functools.partial(add_up, 1.0 / tokens, base // share, n_col),
        (VMEM,),
        [((n_dev, share, LANES), BF16, VMEM)],
        [],
        "add_up", 10**6, 2**19,
    )(exchange(parts.reshape(n_dev, share, LANES)))
    totals = exchange(send).reshape(n_dev * share, LANES)
    (grad_pair,) = call(
        functools.partial(close, half),
        (VMEM,) * 4,
        [((rows_dev, cols_dev, c), BF16, VMEM)],
        [vm(sq, F32)],
        "close", 50 * 10**6, 3 * 2**20,
    )(ng, hat, scale, gain)
    grads = call(
        deliver,
        (VMEM,),
        [((c, 2 * hidden), F32, VMEM)] * 2
        + [((c, c), F32, VMEM), ((hidden, c), F32, VMEM), ((4, c), F32, VMEM)],
        [],
        "deliver", 10**6, 2**20,
    )(totals)
    return (update, grad_pair) + tuple(grads)


def solution(mesh):
    return jax.shard_map(
        per_device,
        mesh=mesh,
        in_specs=(P("row", "col", None), P("row", "col", None)) + (P(),) * 9,
        out_specs=(P("row", "col", None), P("row", "col", None), P(), P(), P(), P(), P()),
        check_vma=False,
    )
```

```python
import functools

import jax
import jax.numpy as jnp
from jax import lax
from jax.experimental import pallas as pl
from jax.experimental.pallas import tpu as pltpu
from jax.sharding import PartitionSpec as P

EPS = 1e-05
BOTH = ("row", "col")
LANES = 128
F32, BF16 = jnp.float32, jnp.bfloat16
NN = (((1,), (0,)), ((), ()))
NT = (((1,), (1,)), ((), ()))
TN = (((0,), (0,)), ((), ()))
VMEM = pl.BlockSpec(memory_space=pltpu.VMEM)
SMEM = pl.BlockSpec(memory_space=pltpu.SMEM)
HBM = pl.BlockSpec(memory_space=pltpu.HBM)
GROUPS = 4


def dot(a, b, dims=NN):
    return lax.dot_general(a, b, dims, preferred_element_type=F32)


def call(body, ins, outs, scratch, name, flops, moved):
    run = pl.pallas_call(
        body,
        in_specs=list(ins),
        out_shape=tuple(
            pltpu.HBM(s, d) if spec is HBM else jax.ShapeDtypeStruct(s, d) for s, d, spec in outs
        ),
        out_specs=tuple(spec for _, _, spec in outs),
        scratch_shapes=scratch,
        name=name,
        compiler_params=pltpu.CompilerParams(vmem_limit_bytes=20 * 2**20),
        cost_estimate=pl.CostEstimate(flops=flops, bytes_accessed=moved, transcendentals=0),
    )

    def placed(*args):
        return run(
            *[
                pltpu.with_memory_space_constraint(x, pltpu.HBM) if spec is HBM else x
                for x, spec in zip(args, ins, strict=True)
            ]
        )

    return placed


def begin(source, target, sem):
    copy = pltpu.make_async_copy(source, target, sem)
    copy.start()
    return copy


def finish_all(copies):
    for copy in copies:
        copy.wait()


def span(g, size):
    return pl.ds(g * size, size)


def exchange(blocks):
    return lax.all_to_all(blocks, BOTH, split_axis=0, concat_axis=0, tiled=True)


def swap_halves(a, b):
    half = LANES // 2
    first = jnp.concatenate([a[:, :half], b[:, :half]], axis=1)
    second = jnp.concatenate([a[:, half:], b[:, half:]], axis=1)
    return first, second


def column(row):
    return jnp.broadcast_to(row, (LANES, row.shape[1])).T


def flip(weight):
    return weight.astype(F32).T.astype(BF16)


def token_tile(ref, p, half):
    return jnp.concatenate([ref[p], ref[half + p]], axis=0)


def mask_row(length, p, half, cols):
    lane = lax.broadcasted_iota(jnp.int32, (1, LANES), 1)
    second = (lane >= cols).astype(jnp.int32)
    row = lax.axis_index("row") * (2 * half) + p + half * second
    col = lax.axis_index("col") * cols + lane - cols * second
    return ((row < length[0]) & (col < length[0])).astype(F32)


def normal(x, axis):
    center = x - jnp.mean(x, axis=axis, keepdims=True)
    inverse = lax.rsqrt(jnp.mean(center * center, axis=axis, keepdims=True) + EPS)
    return center * inverse, inverse


def project(half, hidden, length, pair_h, gain_h, bias_h, lw_h, rw_h, send, nt_out, pair, gain, bias, w, wt, gb, ls, rs, sems):
    n_dev, _, per, _ = send.shape
    cols = pair.shape[1]
    step_rows = half // GROUPS
    small = [
        begin(lw_h, w.at[0], sems.at[0]),
        begin(rw_h, w.at[1], sems.at[1]),
        begin(gain_h, gain, sems.at[2]),
        begin(bias_h, bias, sems.at[3]),
    ]
    tiles = []
    for g in range(GROUPS):
        for k in (0, 1):
            at = pl.ds(k * half + g * step_rows, step_rows)
            tiles.append(begin(pair_h.at[at], pair.at[at], sems.at[4 + 2 * g + k]))
    finish_all(small)
    wt[0] = flip(w[0])
    wt[1] = flip(w[1])
    gb[0] = column(gain[...])
    gb[1] = column(bias[...])

    def step(p, carry):
        x = token_tile(pair, p, half).astype(F32).T
        hat, _ = normal(x, 0)
        nt = (hat * gb[0] + gb[1]).astype(BF16)
        nt_out[:, pl.ds(pl.multiple_of(p * LANES, LANES), LANES)] = nt
        mask = mask_row(length, p, half, cols)
        for side, scr in ((0, ls), (1, rs)):
            proj = dot(wt[side], nt)
            act = mask * jax.nn.sigmoid(proj[hidden:]) * proj[:hidden]
            scr[pl.ds(p, hidden, stride=half), :] = act
        return carry

    for g in range(GROUPS):
        finish_all(tiles[2 * g : 2 * g + 2])
        lax.fori_loop(g * step_rows, (g + 1) * step_rows, step, 0, unroll=4)

    def pack(d, carry):
        at = pl.ds(pl.multiple_of(d * per, per), per)
        send[d, 0] = ls[at, :].astype(BF16)
        send[d, 1] = rs[at, :].astype(BF16)
        return carry

    lax.fori_loop(0, n_dev, pack, 0, unroll=4)


def prepare(half, hidden, length, pair, cot, nt_in, lw, rw, gw, gate_out, cot_out, coef, hat_out, scale_out, wt, gwt):
    cols = pair.shape[1]
    wt[0] = flip(lw[...])
    wt[1] = flip(rw[...])
    gwt[...] = flip(gw[...])

    def step(p, carry):
        at = pl.ds(pl.multiple_of(p * LANES, LANES), LANES)
        x = token_tile(pair, p, half).astype(F32).T
        hat, inverse = normal(x, 0)
        hat_out[:, at] = hat
        scale_out[:, at] = jnp.broadcast_to(inverse, (8, LANES))
        cot_out[:, at] = token_tile(cot, p, half).astype(F32).T.astype(BF16)
        nt = nt_in[:, at]
        gate_out[:, at] = jax.nn.sigmoid(dot(gwt[...], nt))
        mask = mask_row(length, p, half, cols)
        for side in (0, 1):
            proj = dot(wt[side], nt)
            sig = jax.nn.sigmoid(proj[hidden:])
            coef[2 * side, :, at] = mask * sig
            coef[2 * side + 1, :, at] = mask * proj[:hidden] * sig * (1.0 - sig)
        return carry

    lax.fori_loop(0, half, step, 0, unroll=2)


def gather_whole(n_row, n_col, half, read, write):
    for r in range(n_row):
        for m in range(n_col // 2):
            first, second = swap_halves(read(r * n_col + 2 * m), read(r * n_col + 2 * m + 1))
            write(2 * r * half, m * LANES, first)
            write((2 * r + 1) * half, m * LANES, second)


def scatter_tiles(n_row, n_col, half, whole, write):
    for r in range(n_row):
        for m in range(n_col // 2):
            at = slice(m * LANES, (m + 1) * LANES)
            a = whole[2 * r * half : (2 * r + 1) * half, at]
            b = whole[(2 * r + 1) * half : (2 * r + 2) * half, at]
            first, second = swap_halves(a, b)
            write(r * n_col + 2 * m, first)
            write(r * n_col + 2 * m + 1, second)


def multiply(n_row, n_col, half, recv, send_h, left, right, acc, send, sems):
    def step(h, carry):
        at = pl.ds(pl.multiple_of(h * half, half), half)
        for side, out in ((0, left), (1, right)):

            def write(row, lane, block, out=out):
                out[h, row : row + half, lane : lane + LANES] = block

            gather_whole(n_row, n_col, half, lambda d, side=side: recv[d, side, at, :], write)
        acc[h] = dot(left[h], right[h], NT)

        def put(d, block):
            send[d, at, :] = block.astype(BF16)

        scatter_tiles(n_row, n_col, half, acc.at[h], put)
        begin(send.at[:, at], send_h.at[:, at], sems.at[h])
        return carry

    own = left.shape[0]
    lax.fori_loop(0, own, step, 0, unroll=True)
    for h in range(own):
        at = span(h, half)
        pltpu.make_async_copy(send.at[:, at], send_h.at[:, at], sems.at[h]).wait()


def multiply_back(n_row, n_col, half, recv, left, right, send_h, grad, acc, send, sems):
    def step(h, carry):
        at = pl.ds(pl.multiple_of(h * half, half), half)

        def write(row, lane, block):
            grad[h, row : row + half, lane : lane + LANES] = block

        gather_whole(n_row, n_col, half, lambda d: recv[d, at, :], write)
        acc[h, 0] = dot(grad[h], right[h], NN)
        acc[h, 1] = dot(grad[h], left[h], TN)
        for side in (0, 1):

            def put(d, block, side=side):
                send[d, side, at, :] = block.astype(BF16)

            scatter_tiles(n_row, n_col, half, acc.at[h, side], put)
        begin(send.at[:, :, at], send_h.at[:, :, at], sems.at[h])
        return carry

    own = left.shape[0]
    lax.fori_loop(0, own, step, 0, unroll=True)
    for h in range(own):
        at = span(h, half)
        pltpu.make_async_copy(send.at[:, :, at], send_h.at[:, :, at], sems.at[h]).wait()


def unpack(recv, scr, side=None):
    n_dev, per = recv.shape[0], recv.shape[-2]

    def step(d, carry):
        at = pl.ds(pl.multiple_of(d * per, per), per)
        block = recv[d] if side is None else recv[d, side]
        scr[at, :] = block.astype(F32)
        return carry

    lax.fori_loop(0, n_dev, step, 0, unroll=4)


def middle(half, hidden, recv, gate_h, cot_h, gain, bias, ow, send, outer_h, og_h, tn_h, sums, gate_in, cot_in, outer_out, og_out, tn_out, scr, owt, gb, sems, out_sems):
    n_dev, per, _ = send.shape
    size = gate_in.shape[1] // GROUPS
    fetched = []
    for g in range(GROUPS):
        at = span(g, size)
        fetched.append(begin(gate_h.at[:, at], gate_in.at[:, at], sems.at[2 * g]))
        fetched.append(begin(cot_h.at[:, at], cot_in.at[:, at], sems.at[2 * g + 1]))
    unpack(recv, scr)
    owt[...] = flip(ow[...])
    gb[0] = column(gain[...])
    gb[1] = column(bias[...])
    sums[...] = jnp.zeros_like(sums)

    def step(p, carry):
        at = pl.ds(pl.multiple_of(p * LANES, LANES), LANES)
        rows = pl.ds(p, hidden, stride=half)
        hat, scale = normal(scr[rows, :], 0)
        tn = (hat * gb[0] + gb[1]).astype(BF16)
        tn_out[:, at] = tn
        outer = dot(owt[...], tn)
        gate = gate_in[:, at]
        up = cot_in[:, at].astype(F32)
        outer_out[:, at] = outer
        og = (up * gate).astype(BF16)
        og_out[:, at] = og
        tg = dot(ow[...], og)
        sums[0] += tg * hat
        sums[1] += tg
        hg = tg * gb[0]
        back = hg - jnp.mean(hg, axis=0, keepdims=True)
        back = back - hat * jnp.mean(hg * hat, axis=0, keepdims=True)
        scr[rows, :] = scale * back
        return carry

    stored = []
    saved = ((outer_out, outer_h), (og_out, og_h), (tn_out, tn_h))
    for g in range(GROUPS):
        finish_all(fetched[2 * g : 2 * g + 2])
        count = half // GROUPS
        lax.fori_loop(g * count, (g + 1) * count, step, 0, unroll=4)
        at = span(g, size)
        for k, (source, target) in enumerate(saved):
            stored.append(begin(source.at[:, at], target.at[:, at], out_sems.at[3 * g + k]))

    def pack(d, carry):
        at = pl.ds(pl.multiple_of(d * per, per), per)
        send[d] = scr[at, :].astype(BF16)
        return carry

    lax.fori_loop(0, n_dev, pack, 0, unroll=4)
    finish_all(stored)


def fold(x):
    return jnp.sum(x.T, axis=0, keepdims=True)


def settle(half, outer_h, gate_h, cot_h, og_h, tn_h, nt, sums, update, gg_h, early, norms, outer, gate, cot, og, tn, gg, sems):
    pairs = ((outer_h, outer), (gate_h, gate), (cot_h, cot), (og_h, og), (tn_h, tn))
    finish_all([begin(a, b, sems.at[k]) for k, (a, b) in enumerate(pairs)])

    def step(p, carry):
        at = pl.ds(pl.multiple_of(p * LANES, LANES), LANES)
        g, o = gate[:, at], outer[:, at]
        tile = (g * o).T.astype(BF16)
        cols = update.shape[1]
        update[p] = tile[:cols]
        update[half + p] = tile[cols:]
        gg[:, at] = (cot[:, at].astype(F32) * o * g * (1.0 - g)).astype(BF16)
        return carry

    lax.fori_loop(0, half, step, 0, unroll=2)
    stored = begin(gg, gg_h, sems.at[len(pairs)])
    early[0] = dot(nt[...], gg[...], NT)
    early[1] = dot(tn[...], og[...], NT)
    norms[0:1] = fold(sums[0])
    norms[1:2] = fold(sums[1])
    stored.wait()


def finish(half, hidden, recv, coef_h, nt, early, parts, comb_h, coef, comb, scr, sems, out_sems):
    size = nt.shape[1] // GROUPS
    fetched = []
    for g in range(GROUPS):
        at = span(g, size)
        fetched.append(begin(coef_h.at[:, :, at], coef.at[:, :, at], sems.at[g]))
    for side in (0, 1):
        unpack(recv, scr.at[side], side)

    def step(p, carry):
        at = pl.ds(pl.multiple_of(p * LANES, LANES), LANES)
        rows = pl.ds(p, hidden, stride=half)
        for side in (0, 1):
            part = scr[side, rows, :]
            comb[side, :hidden, at] = (part * coef[2 * side, :, at]).astype(BF16)
            comb[side, hidden:, at] = (part * coef[2 * side + 1, :, at]).astype(BF16)
        return carry

    stored = []
    for g in range(GROUPS):
        fetched[g].wait()
        count = half // GROUPS
        lax.fori_loop(g * count, (g + 1) * count, step, 0, unroll=4)
        at = span(g, size)
        stored.append(begin(comb.at[:, :, at], comb_h.at[:, :, at], out_sems.at[g]))
    c = nt.shape[0]
    base = 5 * c + hidden
    for side in (0, 1):
        grad = dot(nt[...], comb[side], NT)
        parts[2 * side * c : (2 * side + 1) * c] = grad[:, :hidden].astype(BF16)
        parts[(2 * side + 1) * c : (2 * side + 2) * c] = grad[:, hidden:].astype(BF16)
    parts[4 * c : 5 * c] = early[0].astype(BF16)
    parts[5 * c : base] = early[1].astype(BF16)
    if parts.shape[0] > base:
        parts[base:] = jnp.zeros((parts.shape[0] - base, LANES), BF16)
    finish_all(stored)


def close(half, comb_h, gg_h, hat_h, scale, gain, lw, rw, gw, early_norms, grad_pair, pairs, comb, gg, hat, sums, gb, sems):
    size = gg.shape[1] // GROUPS
    fetched = []
    for g in range(GROUPS):
        at = span(g, size)
        fetched.append(begin(comb_h.at[:, :, at], comb.at[:, :, at], sems.at[3 * g]))
        fetched.append(begin(gg_h.at[:, at], gg.at[:, at], sems.at[3 * g + 1]))
        fetched.append(begin(hat_h.at[:, at], hat.at[:, at], sems.at[3 * g + 2]))
    gb[...] = column(gain[...])
    sums[...] = jnp.zeros_like(sums)
    cols = grad_pair.shape[1]

    def step(p, carry):
        at = pl.ds(pl.multiple_of(p * LANES, LANES), LANES)
        h = hat[:, at]
        ng = dot(gw[...], gg[:, at]) + dot(lw[...], comb[0, :, at]) + dot(rw[...], comb[1, :, at])
        sums[0] += ng * h
        sums[1] += ng
        q = ng * gb[...]
        back = q - jnp.mean(q, axis=0, keepdims=True)
        back = back - h * jnp.mean(q * h, axis=0, keepdims=True)
        tile = (scale[0:1, at] * back).T.astype(BF16)
        grad_pair[p] = tile[:cols]
        grad_pair[half + p] = tile[cols:]
        return carry

    for g in range(GROUPS):
        finish_all(fetched[3 * g : 3 * g + 3])
        count = half // GROUPS
        lax.fori_loop(g * count, (g + 1) * count, step, 0, unroll=2)
    exact = jnp.concatenate([fold(sums[0]), fold(sums[1]), early_norms[0:2]], axis=0)
    high = exact.astype(BF16)
    pairs[...] = jnp.concatenate([high, (exact - high.astype(F32)).astype(BF16)], axis=0)


def add_up(scale, recv, pairs, send):
    n_dev, share, _ = recv.shape
    mine = (scale * jnp.sum(recv[...].astype(F32), axis=0)).astype(BF16)
    own = pairs[...]
    for d in range(n_dev):
        send[d, :share] = mine
        send[d, share:] = own


def deliver(scale, recv, left, right, gating, output, norms, flat):
    c = left.shape[0]
    n_dev, share = recv.shape[0], recv.shape[1] - 8
    total = jnp.zeros((8, LANES), F32)
    for d in range(n_dev):
        flat[d * share : (d + 1) * share] = recv[d, :share].astype(F32)
        total = total + recv[d, share:].astype(F32)
    for k, out in ((0, left), (2, right)):
        out[:, :LANES] = flat[k * c : (k + 1) * c]
        out[:, LANES:] = flat[(k + 1) * c : (k + 2) * c]
    gating[...] = flat[4 * c : 5 * c]
    output[...] = flat[5 * c : 5 * c + output.shape[0]]
    norms[...] = scale * (total[0:4] + total[4:8])


def per_device(
    pair,
    cotangent,
    length,
    norm_gain,
    norm_bias,
    left_weight,
    right_weight,
    gate_weight,
    out_gain,
    out_bias,
    out_weight,
):
    n_row = lax.axis_size("row")
    n_col = lax.axis_size("col")
    n_dev = n_row * n_col
    rows_dev, cols_dev, c = pair.shape
    tokens = rows_dev * n_row
    hidden = out_weight.shape[0]
    own = hidden // n_dev
    half = rows_dev * cols_dev // LANES
    wide = half * LANES
    per = own * half
    assert 2 * cols_dev == LANES and rows_dev == 2 * half and c == LANES and hidden == LANES
    gain, bias = norm_gain[None], norm_bias[None]
    o_gain, o_bias = out_gain[None], out_bias[None]
    vm, dma = pltpu.VMEM, pltpu.SemaphoreType.DMA
    sq = (c, LANES)
    rows = hidden * half

    send, nt = call(
        functools.partial(project, half, hidden),
        (SMEM,) + (HBM,) * 5,
        [((n_dev, 2, per, LANES), BF16, VMEM), ((c, wide), BF16, VMEM)],
        [vm(pair.shape, BF16), vm((1, c), F32), vm((1, c), F32), vm((2, c, 2 * hidden), BF16)]
        + [vm((2, 2 * hidden, c), BF16), vm((2,) + sq, F32), vm((rows, LANES), F32)]
        + [vm((rows, LANES), F32), dma((4 + 2 * GROUPS,))],
        "project", 300 * 10**6, 3 * 2**20,
    )(length, pair, gain, bias, left_weight, right_weight)
    both = exchange(send)
    gate, cot, coef, hat, scale = call(
        functools.partial(prepare, half, hidden),
        (SMEM,) + (VMEM,) * 6,
        [((c, wide), F32, VMEM), ((c, wide), BF16, VMEM), ((4, hidden, wide), F32, VMEM)]
        + [((c, wide), F32, VMEM), ((8, wide), F32, VMEM)],
        [vm((2, 2 * hidden, c), BF16), vm((c, c), BF16)],
        "prepare", 400 * 10**6, 9 * 2**20,
    )(length, pair, cotangent, nt, left_weight, right_weight, gate_weight)
    send, left, right = call(
        functools.partial(multiply, n_row, n_col, half),
        (VMEM,),
        [((n_dev, per, LANES), BF16, HBM)] + [((own, tokens, tokens), BF16, VMEM)] * 2,
        [vm((own, tokens, tokens), F32), vm((n_dev, per, LANES), BF16), dma((own,))],
        "multiply", 200 * 10**6, 3 * 2**20,
    )(both)
    tri = exchange(send)
    send, outer, og, tn, sums = call(
        functools.partial(middle, half, hidden),
        (VMEM, HBM, HBM, VMEM, VMEM, VMEM),
        [((n_dev, per, LANES), BF16, VMEM), ((c, wide), F32, HBM)]
        + [((c, wide), BF16, HBM)] * 2 + [((2,) + sq, F32, VMEM)],
        [vm((c, wide), F32), vm((c, wide), BF16), vm((c, wide), F32)]
        + [vm((c, wide), BF16)] * 2 + [vm((rows, LANES), F32)]
        + [vm((c, hidden), BF16), vm((2,) + sq, F32), dma((2 * GROUPS,)), dma((3 * GROUPS,))],
        "middle", 200 * 10**6, 6 * 2**20,
    )(tri, gate, cot, o_gain, o_bias, out_weight)
    grad = exchange(send)
    update, gg, early, early_norms = call(
        functools.partial(settle, half),
        (HBM,) * 5 + (VMEM,) * 2,
        [((rows_dev, cols_dev, c), BF16, VMEM), ((c, wide), BF16, HBM)]
        + [((2,) + sq, F32, VMEM), ((8, LANES), F32, VMEM)],
        [vm((c, wide), F32)] * 2 + [vm((c, wide), BF16)] * 4 + [dma((6,))],
        "settle", 200 * 10**6, 4 * 2**20,
    )(outer, gate, cot, og, tn, nt, sums)
    (send,) = call(
        functools.partial(multiply_back, n_row, n_col, half),
        (VMEM,) * 3,
        [((n_dev, 2, per, LANES), BF16, HBM)],
        [vm((own, tokens, tokens), BF16), vm((own, 2, tokens, tokens), F32)]
        + [vm((n_dev, 2, per, LANES), BF16), dma((own,))],
        "multiply_back", 300 * 10**6, 3 * 2**20,
    )(grad, left, right)
    back = exchange(send)
    share = -(-(5 * c + hidden) // (n_dev * 8)) * 8
    parts, comb = call(
        functools.partial(finish, half, hidden),
        (VMEM, HBM, VMEM, VMEM),
        [((n_dev * share, LANES), BF16, VMEM), ((2, 2 * hidden, wide), BF16, HBM)],
        [vm((4, hidden, wide), F32), vm((2, 2 * hidden, wide), BF16), vm((2, rows, LANES), F32)]
        + [dma((GROUPS,)), dma((GROUPS,))],
        "finish", 300 * 10**6, 8 * 2**20,
    )(back, coef, nt, early)
    summed = exchange(parts.reshape(n_dev, share, LANES))
    grad_pair, pairs = call(
        functools.partial(close, half),
        (HBM,) * 3 + (VMEM,) * 6,
        [((rows_dev, cols_dev, c), BF16, VMEM), ((8, LANES), BF16, VMEM)],
        [vm((2, 2 * hidden, wide), BF16), vm((c, wide), BF16), vm((c, wide), F32)]
        + [vm((2,) + sq, F32), vm(sq, F32), dma((3 * GROUPS,))],
        "close", 300 * 10**6, 6 * 2**20,
    )(comb, gg, hat, scale, gain, left_weight, right_weight, gate_weight, early_norms)
    (send,) = call(
        functools.partial(add_up, 1.0 / tokens),
        (VMEM, VMEM),
        [((n_dev, share + 8, LANES), BF16, VMEM)],
        [],
        "add_up", 10**6, 2**19,
    )(summed, pairs)
    grads = call(
        functools.partial(deliver, 1.0 / tokens),
        (VMEM,),
        [((c, 2 * hidden), F32, VMEM)] * 2
        + [((c, c), F32, VMEM), ((hidden, c), F32, VMEM), ((4, c), F32, VMEM)],
        [vm((n_dev * share, LANES), F32)],
        "deliver", 10**6, 2**20,
    )(exchange(send))
    return (update, grad_pair) + tuple(grads)


def solution(mesh):
    return jax.shard_map(
        per_device,
        mesh=mesh,
        in_specs=(P("row", "col", None), P("row", "col", None)) + (P(),) * 9,
        out_specs=(P("row", "col", None), P("row", "col", None), P(), P(), P(), P(), P()),
        check_vma=False,
    )
```

```python
import functools

import jax
import jax.numpy as jnp
from jax import lax
from jax.experimental import pallas as pl
from jax.experimental.pallas import tpu as pltpu
from jax.sharding import PartitionSpec as P

EPS = 1e-05
BOTH = ("row", "col")
LANES = 128
F32, BF16 = jnp.float32, jnp.bfloat16
NN = (((1,), (0,)), ((), ()))
NT = (((1,), (1,)), ((), ()))
TN = (((0,), (0,)), ((), ()))
VMEM = pl.BlockSpec(memory_space=pltpu.VMEM)
SMEM = pl.BlockSpec(memory_space=pltpu.SMEM)
HBM = pl.BlockSpec(memory_space=pltpu.HBM)
GROUPS = 4


def dot(a, b, dims=NN):
    return lax.dot_general(a, b, dims, preferred_element_type=F32)


def call(body, ins, outs, scratch, name, flops, moved):
    run = pl.pallas_call(
        body,
        in_specs=list(ins),
        out_shape=tuple(
            pltpu.HBM(s, d) if spec is HBM else jax.ShapeDtypeStruct(s, d) for s, d, spec in outs
        ),
        out_specs=tuple(spec for _, _, spec in outs),
        scratch_shapes=scratch,
        name=name,
        compiler_params=pltpu.CompilerParams(vmem_limit_bytes=20 * 2**20),
        cost_estimate=pl.CostEstimate(flops=flops, bytes_accessed=moved, transcendentals=0),
    )

    def placed(*args):
        return run(
            *[
                pltpu.with_memory_space_constraint(x, pltpu.HBM) if spec is HBM else x
                for x, spec in zip(args, ins, strict=True)
            ]
        )

    return placed


def begin(source, target, sem):
    copy = pltpu.make_async_copy(source, target, sem)
    copy.start()
    return copy


def finish_all(copies):
    for copy in copies:
        copy.wait()


def span(g, size):
    return pl.ds(g * size, size)


def exchange(blocks):
    return lax.all_to_all(blocks, BOTH, split_axis=0, concat_axis=0, tiled=True)


def swap_halves(a, b):
    half = LANES // 2
    first = jnp.concatenate([a[:, :half], b[:, :half]], axis=1)
    second = jnp.concatenate([a[:, half:], b[:, half:]], axis=1)
    return first, second


def column(row):
    return jnp.broadcast_to(row, (LANES, row.shape[1])).T


def flip(weight):
    return weight.astype(F32).T.astype(BF16)


def token_tile(ref, p, half):
    return jnp.concatenate([ref[p], ref[half + p]], axis=0)


def mask_row(length, p, half, cols):
    lane = lax.broadcasted_iota(jnp.int32, (1, LANES), 1)
    second = (lane >= cols).astype(jnp.int32)
    row = lax.axis_index("row") * (2 * half) + p + half * second
    col = lax.axis_index("col") * cols + lane - cols * second
    return ((row < length[0]) & (col < length[0])).astype(F32)


def normal(x, axis):
    center = x - jnp.mean(x, axis=axis, keepdims=True)
    inverse = lax.rsqrt(jnp.mean(center * center, axis=axis, keepdims=True) + EPS)
    return center * inverse, inverse


def project(half, hidden, length, pair_h, gain_h, bias_h, lw_h, rw_h, send, nt_out, pair, gain, bias, w, wt, gb, ls, rs, sems):
    n_dev, _, per, _ = send.shape
    cols = pair.shape[1]
    step_rows = half // GROUPS
    small = [
        begin(lw_h, w.at[0], sems.at[0]),
        begin(rw_h, w.at[1], sems.at[1]),
        begin(gain_h, gain, sems.at[2]),
        begin(bias_h, bias, sems.at[3]),
    ]
    tiles = []
    for g in range(GROUPS):
        for k in (0, 1):
            at = pl.ds(k * half + g * step_rows, step_rows)
            tiles.append(begin(pair_h.at[at], pair.at[at], sems.at[4 + 2 * g + k]))
    finish_all(small)
    wt[0] = flip(w[0])
    wt[1] = flip(w[1])
    gb[0] = column(gain[...])
    gb[1] = column(bias[...])

    def step(p, carry):
        x = token_tile(pair, p, half).astype(F32).T
        hat, _ = normal(x, 0)
        nt = (hat * gb[0] + gb[1]).astype(BF16)
        nt_out[:, pl.ds(pl.multiple_of(p * LANES, LANES), LANES)] = nt
        mask = mask_row(length, p, half, cols)
        for side, scr in ((0, ls), (1, rs)):
            proj = dot(wt[side], nt)
            act = mask * jax.nn.sigmoid(proj[hidden:]) * proj[:hidden]
            scr[pl.ds(p, hidden, stride=half + 1), :] = act
        return carry

    for g in range(GROUPS):
        finish_all(tiles[2 * g : 2 * g + 2])
        lax.fori_loop(g * step_rows, (g + 1) * step_rows, step, 0, unroll=4)

    def pack(d, carry):
        for k in range(per // half):
            at = pl.ds((d * (per // half) + k) * (half + 1), half)
            to = slice(k * half, (k + 1) * half)
            send[d, 0, to] = ls[at, :].astype(BF16)
            send[d, 1, to] = rs[at, :].astype(BF16)
        return carry

    lax.fori_loop(0, n_dev, pack, 0, unroll=4)


def prepare(half, hidden, length, pair, cot, nt_in, lw, rw, gw, gate_out, cot_out, coef, hat_out, scale_out, wt, gwt):
    cols = pair.shape[1]
    wt[0] = flip(lw[...])
    wt[1] = flip(rw[...])
    gwt[...] = flip(gw[...])

    def step(p, carry):
        at = pl.ds(pl.multiple_of(p * LANES, LANES), LANES)
        x = token_tile(pair, p, half).astype(F32).T
        hat, inverse = normal(x, 0)
        hat_out[:, at] = hat
        scale_out[:, at] = jnp.broadcast_to(inverse, (8, LANES))
        cot_out[:, at] = token_tile(cot, p, half).astype(F32).T.astype(BF16)
        nt = nt_in[:, at]
        gate_out[:, at] = jax.nn.sigmoid(dot(gwt[...], nt))
        mask = mask_row(length, p, half, cols)
        for side in (0, 1):
            proj = dot(wt[side], nt)
            sig = jax.nn.sigmoid(proj[hidden:])
            coef[2 * side, :, at] = (mask * sig).astype(BF16)
            slope = mask * proj[:hidden] * sig * (1.0 - sig)
            coef[2 * side + 1, :, at] = slope.astype(BF16)
        return carry

    lax.fori_loop(0, half, step, 0, unroll=2)


def gather_whole(n_row, n_col, half, read, write):
    for r in range(n_row):
        for m in range(n_col // 2):
            first, second = swap_halves(read(r * n_col + 2 * m), read(r * n_col + 2 * m + 1))
            write(2 * r * half, m * LANES, first)
            write((2 * r + 1) * half, m * LANES, second)


def scatter_tiles(n_row, n_col, half, whole, write):
    for r in range(n_row):
        for m in range(n_col // 2):
            at = slice(m * LANES, (m + 1) * LANES)
            a = whole[2 * r * half : (2 * r + 1) * half, at]
            b = whole[(2 * r + 1) * half : (2 * r + 2) * half, at]
            first, second = swap_halves(a, b)
            write(r * n_col + 2 * m, first)
            write(r * n_col + 2 * m + 1, second)


def multiply(n_row, n_col, half, recv, send_h, left, right, acc, send, sems):
    def step(h, carry):
        at = pl.ds(pl.multiple_of(h * half, half), half)
        for side, out in ((0, left), (1, right)):

            def write(row, lane, block, out=out):
                out[h, row : row + half, lane : lane + LANES] = block

            gather_whole(n_row, n_col, half, lambda d, side=side: recv[d, side, at, :], write)
        acc[h] = dot(left[h], right[h], NT)

        def put(d, block):
            send[d, at, :] = block.astype(BF16)

        scatter_tiles(n_row, n_col, half, acc.at[h], put)
        begin(send.at[:, at], send_h.at[:, at], sems.at[h])
        return carry

    own = left.shape[0]
    lax.fori_loop(0, own, step, 0, unroll=True)
    for h in range(own):
        at = span(h, half)
        pltpu.make_async_copy(send.at[:, at], send_h.at[:, at], sems.at[h]).wait()


def multiply_back(n_row, n_col, half, recv, left, right, send_h, grad, acc, send, sems):
    def step(h, carry):
        at = pl.ds(pl.multiple_of(h * half, half), half)

        def write(row, lane, block):
            grad[h, row : row + half, lane : lane + LANES] = block

        gather_whole(n_row, n_col, half, lambda d: recv[d, at, :], write)
        acc[h, 0] = dot(grad[h], right[h], NN)
        acc[h, 1] = dot(grad[h], left[h], TN)
        for side in (0, 1):

            def put(d, block, side=side):
                send[d, side, at, :] = block.astype(BF16)

            scatter_tiles(n_row, n_col, half, acc.at[h, side], put)
        begin(send.at[:, :, at], send_h.at[:, :, at], sems.at[h])
        return carry

    own = left.shape[0]
    lax.fori_loop(0, own, step, 0, unroll=True)
    for h in range(own):
        at = span(h, half)
        pltpu.make_async_copy(send.at[:, :, at], send_h.at[:, :, at], sems.at[h]).wait()


def unpack(half, recv, scr, side=None):
    n_dev, per = recv.shape[0], recv.shape[-2]

    def step(d, carry):
        block = (recv[d] if side is None else recv[d, side]).astype(F32)
        for k in range(per // half):
            at = pl.ds((d * (per // half) + k) * (half + 1), half)
            scr[at, :] = block[k * half : (k + 1) * half]
        return carry

    lax.fori_loop(0, n_dev, step, 0, unroll=4)


def middle(half, hidden, recv, gate_h, cot_h, gain, bias, ow, send, outer_h, og_h, tn_h, sums, gate_in, cot_in, outer_out, og_out, tn_out, scr, owt, gb, sems, out_sems):
    n_dev, per, _ = send.shape
    size = gate_in.shape[1] // GROUPS
    fetched = []
    for g in range(GROUPS):
        at = span(g, size)
        fetched.append(begin(gate_h.at[:, at], gate_in.at[:, at], sems.at[2 * g]))
        fetched.append(begin(cot_h.at[:, at], cot_in.at[:, at], sems.at[2 * g + 1]))
    unpack(half, recv, scr)
    owt[...] = flip(ow[...])
    gb[0] = column(gain[...])
    gb[1] = column(bias[...])
    sums[...] = jnp.zeros_like(sums)

    def step(p, carry):
        at = pl.ds(pl.multiple_of(p * LANES, LANES), LANES)
        rows = pl.ds(p, hidden, stride=half + 1)
        hat, scale = normal(scr[rows, :], 0)
        tn = (hat * gb[0] + gb[1]).astype(BF16)
        tn_out[:, at] = tn
        outer = dot(owt[...], tn)
        gate = gate_in[:, at]
        up = cot_in[:, at].astype(F32)
        outer_out[:, at] = outer
        og = (up * gate).astype(BF16)
        og_out[:, at] = og
        tg = dot(ow[...], og)
        sums[0] += tg * hat
        sums[1] += tg
        hg = tg * gb[0]
        back = hg - jnp.mean(hg, axis=0, keepdims=True)
        back = back - hat * jnp.mean(hg * hat, axis=0, keepdims=True)
        scr[rows, :] = scale * back
        return carry

    stored = []
    saved = ((outer_out, outer_h), (og_out, og_h), (tn_out, tn_h))
    for g in range(GROUPS):
        finish_all(fetched[2 * g : 2 * g + 2])
        count = half // GROUPS
        lax.fori_loop(g * count, (g + 1) * count, step, 0, unroll=4)
        at = span(g, size)
        for k, (source, target) in enumerate(saved):
            stored.append(begin(source.at[:, at], target.at[:, at], out_sems.at[3 * g + k]))

    def pack(d, carry):
        for k in range(per // half):
            at = pl.ds((d * (per // half) + k) * (half + 1), half)
            send[d, k * half : (k + 1) * half] = scr[at, :].astype(BF16)
        return carry

    lax.fori_loop(0, n_dev, pack, 0, unroll=4)
    finish_all(stored)


def fold(x):
    return jnp.sum(x.T, axis=0, keepdims=True)


def settle(half, outer_h, gate_h, cot_h, og_h, tn_h, nt, sums, update, gg_h, early, norms, outer, gate, cot, og, tn, gg, sems):
    pairs = ((outer_h, outer), (gate_h, gate), (cot_h, cot), (og_h, og), (tn_h, tn))
    finish_all([begin(a, b, sems.at[k]) for k, (a, b) in enumerate(pairs)])

    def step(p, carry):
        at = pl.ds(pl.multiple_of(p * LANES, LANES), LANES)
        g, o = gate[:, at], outer[:, at]
        tile = (g * o).T.astype(BF16)
        cols = update.shape[1]
        update[p] = tile[:cols]
        update[half + p] = tile[cols:]
        gg[:, at] = (cot[:, at].astype(F32) * o * g * (1.0 - g)).astype(BF16)
        return carry

    lax.fori_loop(0, half, step, 0, unroll=2)
    stored = begin(gg, gg_h, sems.at[len(pairs)])
    early[0] = dot(nt[...], gg[...], NT)
    early[1] = dot(tn[...], og[...], NT)
    norms[0:1] = fold(sums[0])
    norms[1:2] = fold(sums[1])
    stored.wait()


def finish(half, hidden, recv, coef_h, nt, early, parts, comb_h, coef, comb, scr, total, sems, out_sems):
    size = nt.shape[1] // GROUPS
    fetched = []
    for g in range(GROUPS):
        at = span(g, size)
        fetched.append(begin(coef_h.at[:, :, at], coef.at[:, :, at], sems.at[g]))
    for side in (0, 1):
        unpack(half, recv, scr.at[side], side)

    def step(p, carry):
        at = pl.ds(pl.multiple_of(p * LANES, LANES), LANES)
        rows = pl.ds(p, hidden, stride=half + 1)
        for side in (0, 1):
            part = scr[side, rows, :]
            comb[side, :hidden, at] = (part * coef[2 * side, :, at].astype(F32)).astype(BF16)
            comb[side, hidden:, at] = (part * coef[2 * side + 1, :, at].astype(F32)).astype(BF16)
        return carry

    stored = []
    for g in range(GROUPS):
        fetched[g].wait()
        count = half // GROUPS
        lax.fori_loop(g * count, (g + 1) * count, step, 0, unroll=4)
        at = span(g, size)
        stored.append(begin(comb.at[:, :, at], comb_h.at[:, :, at], out_sems.at[g]))
        here = slice(g * size, (g + 1) * size)
        for side in (0, 1):
            part = dot(nt[:, here], comb[side, :, here], NT)
            total[side] = part if g == 0 else total[side] + part
    c = nt.shape[0]
    base = 5 * c + hidden
    for side in (0, 1):
        grad = total[side]
        parts[2 * side * c : (2 * side + 1) * c] = grad[:, :hidden].astype(BF16)
        parts[(2 * side + 1) * c : (2 * side + 2) * c] = grad[:, hidden:].astype(BF16)
    parts[4 * c : 5 * c] = early[0].astype(BF16)
    parts[5 * c : base] = early[1].astype(BF16)
    if parts.shape[0] > base:
        parts[base:] = jnp.zeros((parts.shape[0] - base, LANES), BF16)
    finish_all(stored)


def close(half, comb_h, gg_h, hat_h, scale, gain, lw, rw, gw, early_norms, grad_pair, pairs, comb, gg, hat, sums, gb, sems):
    size = gg.shape[1] // GROUPS
    fetched = []
    for g in range(GROUPS):
        at = span(g, size)
        fetched.append(begin(comb_h.at[:, :, at], comb.at[:, :, at], sems.at[3 * g]))
        fetched.append(begin(gg_h.at[:, at], gg.at[:, at], sems.at[3 * g + 1]))
        fetched.append(begin(hat_h.at[:, at], hat.at[:, at], sems.at[3 * g + 2]))
    gb[...] = column(gain[...])
    sums[...] = jnp.zeros_like(sums)
    cols = grad_pair.shape[1]

    def step(p, carry):
        at = pl.ds(pl.multiple_of(p * LANES, LANES), LANES)
        h = hat[:, at]
        ng = dot(gw[...], gg[:, at]) + dot(lw[...], comb[0, :, at]) + dot(rw[...], comb[1, :, at])
        sums[0] += ng * h
        sums[1] += ng
        q = ng * gb[...]
        back = q - jnp.mean(q, axis=0, keepdims=True)
        back = back - h * jnp.mean(q * h, axis=0, keepdims=True)
        tile = (scale[0:1, at] * back).T.astype(BF16)
        grad_pair[p] = tile[:cols]
        grad_pair[half + p] = tile[cols:]
        return carry

    for g in range(GROUPS):
        finish_all(fetched[3 * g : 3 * g + 3])
        count = half // GROUPS
        lax.fori_loop(g * count, (g + 1) * count, step, 0, unroll=2)
    exact = jnp.concatenate([fold(sums[0]), fold(sums[1]), early_norms[0:2]], axis=0)
    high = exact.astype(BF16)
    pairs[...] = jnp.concatenate([high, (exact - high.astype(F32)).astype(BF16)], axis=0)


def add_up(scale, recv, pairs, send):
    n_dev, share, _ = recv.shape
    mine = (scale * jnp.sum(recv[...].astype(F32), axis=0)).astype(BF16)
    own = pairs[...]
    for d in range(n_dev):
        send[d, :share] = mine
        send[d, share:] = own


def deliver(scale, recv, left, right, gating, output, norms, flat):
    c = left.shape[0]
    n_dev, share = recv.shape[0], recv.shape[1] - 8
    total = jnp.zeros((8, LANES), F32)
    for d in range(n_dev):
        flat[d * share : (d + 1) * share] = recv[d, :share].astype(F32)
        total = total + recv[d, share:].astype(F32)
    for k, out in ((0, left), (2, right)):
        out[:, :LANES] = flat[k * c : (k + 1) * c]
        out[:, LANES:] = flat[(k + 1) * c : (k + 2) * c]
    gating[...] = flat[4 * c : 5 * c]
    output[...] = flat[5 * c : 5 * c + output.shape[0]]
    norms[...] = scale * (total[0:4] + total[4:8])


def per_device(
    pair,
    cotangent,
    length,
    norm_gain,
    norm_bias,
    left_weight,
    right_weight,
    gate_weight,
    out_gain,
    out_bias,
    out_weight,
):
    n_row = lax.axis_size("row")
    n_col = lax.axis_size("col")
    n_dev = n_row * n_col
    rows_dev, cols_dev, c = pair.shape
    tokens = rows_dev * n_row
    hidden = out_weight.shape[0]
    own = hidden // n_dev
    half = rows_dev * cols_dev // LANES
    wide = half * LANES
    per = own * half
    assert 2 * cols_dev == LANES and rows_dev == 2 * half and c == LANES and hidden == LANES
    gain, bias = norm_gain[None], norm_bias[None]
    o_gain, o_bias = out_gain[None], out_bias[None]
    vm, dma = pltpu.VMEM, pltpu.SemaphoreType.DMA
    sq = (c, LANES)
    rows = hidden * (half + 1)

    send, nt = call(
        functools.partial(project, half, hidden),
        (SMEM,) + (HBM,) * 5,
        [((n_dev, 2, per, LANES), BF16, VMEM), ((c, wide), BF16, VMEM)],
        [vm(pair.shape, BF16), vm((1, c), F32), vm((1, c), F32), vm((2, c, 2 * hidden), BF16)]
        + [vm((2, 2 * hidden, c), BF16), vm((2,) + sq, F32), vm((rows, LANES), F32)]
        + [vm((rows, LANES), F32), dma((4 + 2 * GROUPS,))],
        "project", 300 * 10**6, 3 * 2**20,
    )(length, pair, gain, bias, left_weight, right_weight)
    both = exchange(send)
    gate, cot, coef, hat, scale = call(
        functools.partial(prepare, half, hidden),
        (SMEM,) + (VMEM,) * 6,
        [((c, wide), F32, VMEM), ((c, wide), BF16, VMEM), ((4, hidden, wide), BF16, VMEM)]
        + [((c, wide), F32, VMEM), ((8, wide), F32, VMEM)],
        [vm((2, 2 * hidden, c), BF16), vm((c, c), BF16)],
        "prepare", 400 * 10**6, 9 * 2**20,
    )(length, pair, cotangent, nt, left_weight, right_weight, gate_weight)
    send, left, right = call(
        functools.partial(multiply, n_row, n_col, half),
        (VMEM,),
        [((n_dev, per, LANES), BF16, HBM)] + [((own, tokens, tokens), BF16, VMEM)] * 2,
        [vm((own, tokens, tokens), F32), vm((n_dev, per, LANES), BF16), dma((own,))],
        "multiply", 200 * 10**6, 3 * 2**20,
    )(both)
    tri = exchange(send)
    send, outer, og, tn, sums = call(
        functools.partial(middle, half, hidden),
        (VMEM, HBM, HBM, VMEM, VMEM, VMEM),
        [((n_dev, per, LANES), BF16, VMEM), ((c, wide), F32, HBM)]
        + [((c, wide), BF16, HBM)] * 2 + [((2,) + sq, F32, VMEM)],
        [vm((c, wide), F32), vm((c, wide), BF16), vm((c, wide), F32)]
        + [vm((c, wide), BF16)] * 2 + [vm((rows, LANES), F32)]
        + [vm((c, hidden), BF16), vm((2,) + sq, F32), dma((2 * GROUPS,)), dma((3 * GROUPS,))],
        "middle", 200 * 10**6, 6 * 2**20,
    )(tri, gate, cot, o_gain, o_bias, out_weight)
    grad = exchange(send)
    update, gg, early, early_norms = call(
        functools.partial(settle, half),
        (HBM,) * 5 + (VMEM,) * 2,
        [((rows_dev, cols_dev, c), BF16, VMEM), ((c, wide), BF16, HBM)]
        + [((2,) + sq, F32, VMEM), ((8, LANES), F32, VMEM)],
        [vm((c, wide), F32)] * 2 + [vm((c, wide), BF16)] * 4 + [dma((6,))],
        "settle", 200 * 10**6, 4 * 2**20,
    )(outer, gate, cot, og, tn, nt, sums)
    (send,) = call(
        functools.partial(multiply_back, n_row, n_col, half),
        (VMEM,) * 3,
        [((n_dev, 2, per, LANES), BF16, HBM)],
        [vm((own, tokens, tokens), BF16), vm((own, 2, tokens, tokens), F32)]
        + [vm((n_dev, 2, per, LANES), BF16), dma((own,))],
        "multiply_back", 300 * 10**6, 3 * 2**20,
    )(grad, left, right)
    back = exchange(send)
    share = -(-(5 * c + hidden) // (n_dev * 8)) * 8
    parts, comb = call(
        functools.partial(finish, half, hidden),
        (VMEM, HBM, VMEM, VMEM),
        [((n_dev * share, LANES), BF16, VMEM), ((2, 2 * hidden, wide), BF16, HBM)],
        [vm((4, hidden, wide), BF16), vm((2, 2 * hidden, wide), BF16), vm((2, rows, LANES), F32)]
        + [vm((2, c, 2 * hidden), F32), dma((GROUPS,)), dma((GROUPS,))],
        "finish", 300 * 10**6, 8 * 2**20,
    )(back, coef, nt, early)
    summed = exchange(parts.reshape(n_dev, share, LANES))
    grad_pair, pairs = call(
        functools.partial(close, half),
        (HBM,) * 3 + (VMEM,) * 6,
        [((rows_dev, cols_dev, c), BF16, VMEM), ((8, LANES), BF16, VMEM)],
        [vm((2, 2 * hidden, wide), BF16), vm((c, wide), BF16), vm((c, wide), F32)]
        + [vm((2,) + sq, F32), vm(sq, F32), dma((3 * GROUPS,))],
        "close", 300 * 10**6, 6 * 2**20,
    )(comb, gg, hat, scale, gain, left_weight, right_weight, gate_weight, early_norms)
    (send,) = call(
        functools.partial(add_up, 1.0 / tokens),
        (VMEM, VMEM),
        [((n_dev, share + 8, LANES), BF16, VMEM)],
        [],
        "add_up", 10**6, 2**19,
    )(summed, pairs)
    grads = call(
        functools.partial(deliver, 1.0 / tokens),
        (VMEM,),
        [((c, 2 * hidden), F32, VMEM)] * 2
        + [((c, c), F32, VMEM), ((hidden, c), F32, VMEM), ((4, c), F32, VMEM)],
        [vm((n_dev * share, LANES), F32)],
        "deliver", 10**6, 2**20,
    )(exchange(send))
    return (update, grad_pair) + tuple(grads)


def solution(mesh):
    return jax.shard_map(
        per_device,
        mesh=mesh,
        in_specs=(P("row", "col", None), P("row", "col", None)) + (P(),) * 9,
        out_specs=(P("row", "col", None), P("row", "col", None), P(), P(), P(), P(), P()),
        check_vma=False,
    )
```

```python
import functools

import jax
import jax.numpy as jnp
from jax import lax
from jax.experimental import pallas as pl
from jax.experimental.pallas import tpu as pltpu
from jax.sharding import PartitionSpec as P

EPS = 1e-05
BOTH = ("row", "col")
LANES = 128
F32, BF16 = jnp.float32, jnp.bfloat16
NN = (((1,), (0,)), ((), ()))
NT = (((1,), (1,)), ((), ()))
TN = (((0,), (0,)), ((), ()))
VMEM = pl.BlockSpec(memory_space=pltpu.VMEM)
SMEM = pl.BlockSpec(memory_space=pltpu.SMEM)
HBM = pl.BlockSpec(memory_space=pltpu.HBM)
GROUPS = 2


def dot(a, b, dims=NN):
    return lax.dot_general(a, b, dims, preferred_element_type=F32)


def call(body, ins, outs, scratch, name, flops, moved):
    run = pl.pallas_call(
        body,
        in_specs=list(ins),
        out_shape=tuple(
            pltpu.HBM(s, d) if spec is HBM else jax.ShapeDtypeStruct(s, d) for s, d, spec in outs
        ),
        out_specs=tuple(spec for _, _, spec in outs),
        scratch_shapes=scratch,
        name=name,
        compiler_params=pltpu.CompilerParams(vmem_limit_bytes=20 * 2**20),
        cost_estimate=pl.CostEstimate(flops=flops, bytes_accessed=moved, transcendentals=0),
    )

    def placed(*args):
        return run(
            *[
                pltpu.with_memory_space_constraint(x, pltpu.HBM) if spec is HBM else x
                for x, spec in zip(args, ins, strict=True)
            ]
        )

    return placed


def begin(source, target, sem):
    copy = pltpu.make_async_copy(source, target, sem)
    copy.start()
    return copy


def finish_all(copies):
    for copy in copies:
        copy.wait()


def span(g, size):
    return pl.ds(g * size, size)


def exchange(blocks):
    return lax.all_to_all(blocks, BOTH, split_axis=0, concat_axis=0, tiled=True)


def swap_halves(a, b):
    half = LANES // 2
    first = jnp.concatenate([a[:, :half], b[:, :half]], axis=1)
    second = jnp.concatenate([a[:, half:], b[:, half:]], axis=1)
    return first, second


def column(row):
    return jnp.broadcast_to(row, (LANES, row.shape[1])).T


def flip(weight):
    return weight.astype(F32).T.astype(BF16)


def token_tile(ref, p, half):
    return jnp.concatenate([ref[p], ref[half + p]], axis=0)


def mask_row(length, p, half, cols):
    lane = lax.broadcasted_iota(jnp.int32, (1, LANES), 1)
    second = (lane >= cols).astype(jnp.int32)
    row = lax.axis_index("row") * (2 * half) + p + half * second
    col = lax.axis_index("col") * cols + lane - cols * second
    return ((row < length[0]) & (col < length[0])).astype(F32)


def normal(x, axis):
    center = x - jnp.mean(x, axis=axis, keepdims=True)
    inverse = lax.rsqrt(jnp.mean(center * center, axis=axis, keepdims=True) + EPS)
    return center * inverse, inverse


def project(half, hidden, length, pair_h, gain_h, bias_h, lw_h, rw_h, send, nt_out, pair, gain, bias, w, wt, gb, ls, rs, sems):
    n_dev, _, per, _ = send.shape
    cols = pair.shape[1]
    step_rows = half // GROUPS
    small = [
        begin(lw_h, w.at[0], sems.at[0]),
        begin(rw_h, w.at[1], sems.at[1]),
        begin(gain_h, gain, sems.at[2]),
        begin(bias_h, bias, sems.at[3]),
    ]
    tiles = []
    for g in range(GROUPS):
        for k in (0, 1):
            at = pl.ds(k * half + g * step_rows, step_rows)
            tiles.append(begin(pair_h.at[at], pair.at[at], sems.at[4 + 2 * g + k]))
    finish_all(small)
    wt[0] = flip(w[0])
    wt[1] = flip(w[1])
    gb[0] = column(gain[...])
    gb[1] = column(bias[...])

    def step(p, carry):
        x = token_tile(pair, p, half).astype(F32).T
        hat, _ = normal(x, 0)
        nt = (hat * gb[0] + gb[1]).astype(BF16)
        nt_out[:, pl.ds(pl.multiple_of(p * LANES, LANES), LANES)] = nt
        mask = mask_row(length, p, half, cols)
        for side, scr in ((0, ls), (1, rs)):
            proj = dot(wt[side], nt)
            act = mask * jax.nn.sigmoid(proj[hidden:]) * proj[:hidden]
            scr[pl.ds(p, hidden, stride=half + 1), :] = act
        return carry

    for g in range(GROUPS):
        finish_all(tiles[2 * g : 2 * g + 2])
        lax.fori_loop(g * step_rows, (g + 1) * step_rows, step, 0, unroll=8)

    def pack(d, carry):
        for k in range(per // half):
            at = pl.ds((d * (per // half) + k) * (half + 1), half)
            to = slice(k * half, (k + 1) * half)
            send[d, 0, to] = ls[at, :].astype(BF16)
            send[d, 1, to] = rs[at, :].astype(BF16)
        return carry

    lax.fori_loop(0, n_dev, pack, 0, unroll=4)


def prepare(half, hidden, length, pair, cot, nt_in, lw, rw, gw, gate_out, cot_out, coef, hat_out, scale_out, wt, gwt):
    cols = pair.shape[1]
    wt[0] = flip(lw[...])
    wt[1] = flip(rw[...])
    gwt[...] = flip(gw[...])

    def step(p, carry):
        at = pl.ds(pl.multiple_of(p * LANES, LANES), LANES)
        x = token_tile(pair, p, half).astype(F32).T
        hat, inverse = normal(x, 0)
        hat_out[:, at] = hat
        scale_out[:, at] = jnp.broadcast_to(inverse, (8, LANES))
        cot_out[:, at] = token_tile(cot, p, half).astype(F32).T.astype(BF16)
        nt = nt_in[:, at]
        gate_out[:, at] = jax.nn.sigmoid(dot(gwt[...], nt))
        mask = mask_row(length, p, half, cols)
        for side in (0, 1):
            proj = dot(wt[side], nt)
            sig = jax.nn.sigmoid(proj[hidden:])
            coef[2 * side, :, at] = (mask * sig).astype(BF16)
            slope = mask * proj[:hidden] * sig * (1.0 - sig)
            coef[2 * side + 1, :, at] = slope.astype(BF16)
        return carry

    lax.fori_loop(0, half, step, 0, unroll=2)


def gather_whole(n_row, n_col, half, read, write):
    for r in range(n_row):
        for m in range(n_col // 2):
            first, second = swap_halves(read(r * n_col + 2 * m), read(r * n_col + 2 * m + 1))
            write(2 * r * half, m * LANES, first)
            write((2 * r + 1) * half, m * LANES, second)


def scatter_tiles(n_row, n_col, half, whole, write):
    for r in range(n_row):
        for m in range(n_col // 2):
            at = slice(m * LANES, (m + 1) * LANES)
            a = whole[2 * r * half : (2 * r + 1) * half, at]
            b = whole[(2 * r + 1) * half : (2 * r + 2) * half, at]
            first, second = swap_halves(a, b)
            write(r * n_col + 2 * m, first)
            write(r * n_col + 2 * m + 1, second)


def multiply(n_row, n_col, half, recv, send_h, left, right, acc, send, sems):
    def step(h, carry):
        at = pl.ds(pl.multiple_of(h * half, half), half)
        for side, out in ((0, left), (1, right)):

            def write(row, lane, block, out=out):
                out[h, row : row + half, lane : lane + LANES] = block

            gather_whole(n_row, n_col, half, lambda d, side=side: recv[d, side, at, :], write)
        acc[h] = dot(left[h], right[h], NT)

        def put(d, block):
            send[d, at, :] = block.astype(BF16)

        scatter_tiles(n_row, n_col, half, acc.at[h], put)
        begin(send.at[:, at], send_h.at[:, at], sems.at[h])
        return carry

    own = left.shape[0]
    lax.fori_loop(0, own, step, 0, unroll=True)
    for h in range(own):
        at = span(h, half)
        pltpu.make_async_copy(send.at[:, at], send_h.at[:, at], sems.at[h]).wait()


def multiply_back(n_row, n_col, half, recv, left, right, send_h, grad, acc, send, sems):
    def step(h, carry):
        at = pl.ds(pl.multiple_of(h * half, half), half)

        def write(row, lane, block):
            grad[h, row : row + half, lane : lane + LANES] = block

        gather_whole(n_row, n_col, half, lambda d: recv[d, at, :], write)
        acc[h, 0] = dot(grad[h], right[h], NN)
        acc[h, 1] = dot(grad[h], left[h], TN)
        for side in (0, 1):

            def put(d, block, side=side):
                send[d, side, at, :] = block.astype(BF16)

            scatter_tiles(n_row, n_col, half, acc.at[h, side], put)
        begin(send.at[:, :, at], send_h.at[:, :, at], sems.at[h])
        return carry

    own = left.shape[0]
    lax.fori_loop(0, own, step, 0, unroll=True)
    for h in range(own):
        at = span(h, half)
        pltpu.make_async_copy(send.at[:, :, at], send_h.at[:, :, at], sems.at[h]).wait()


def unpack(half, recv, scr, side=None):
    n_dev, per = recv.shape[0], recv.shape[-2]

    def step(d, carry):
        block = (recv[d] if side is None else recv[d, side]).astype(F32)
        for k in range(per // half):
            at = pl.ds((d * (per // half) + k) * (half + 1), half)
            scr[at, :] = block[k * half : (k + 1) * half]
        return carry

    lax.fori_loop(0, n_dev, step, 0, unroll=4)


def middle(half, hidden, recv, gate_h, cot_h, gain, bias, ow, send, tn_h, sums, gate_in, cot_in, tn_out, scr, gb, sems, out_sems):
    n_dev, per, _ = send.shape
    size = gate_in.shape[1] // GROUPS
    fetched = []
    for g in range(GROUPS):
        at = span(g, size)
        fetched.append(begin(gate_h.at[:, at], gate_in.at[:, at], sems.at[2 * g]))
        fetched.append(begin(cot_h.at[:, at], cot_in.at[:, at], sems.at[2 * g + 1]))
    unpack(half, recv, scr)
    gb[0] = column(gain[...])
    gb[1] = column(bias[...])
    sums[...] = jnp.zeros_like(sums)

    def step(p, carry):
        at = pl.ds(pl.multiple_of(p * LANES, LANES), LANES)
        rows = pl.ds(p, hidden, stride=half + 1)
        hat, scale = normal(scr[rows, :], 0)
        tn = (hat * gb[0] + gb[1]).astype(BF16)
        tn_out[:, at] = tn
        gate = gate_in[:, at]
        up = cot_in[:, at].astype(F32)
        og = (up * gate).astype(BF16)
        tg = dot(ow[...], og)
        sums[0] += tg * hat
        sums[1] += tg
        hg = tg * gb[0]
        back = hg - jnp.mean(hg, axis=0, keepdims=True)
        back = back - hat * jnp.mean(hg * hat, axis=0, keepdims=True)
        scr[rows, :] = scale * back
        return carry

    stored = []
    for g in range(GROUPS):
        finish_all(fetched[2 * g : 2 * g + 2])
        count = half // GROUPS
        lax.fori_loop(g * count, (g + 1) * count, step, 0, unroll=8)
        at = span(g, size)
        stored.append(begin(tn_out.at[:, at], tn_h.at[:, at], out_sems.at[g]))

    def pack(d, carry):
        for k in range(per // half):
            at = pl.ds((d * (per // half) + k) * (half + 1), half)
            send[d, k * half : (k + 1) * half] = scr[at, :].astype(BF16)
        return carry

    lax.fori_loop(0, n_dev, pack, 0, unroll=4)
    finish_all(stored)


def fold(x):
    return jnp.sum(x.T, axis=0, keepdims=True)


def settle(half, gate_h, cot_h, tn_h, nt, sums, ow, update, gg_h, early, norms, gate, cot, og, tn, gg, owt, sems):
    owt[...] = flip(ow[...])
    pairs = ((gate_h, gate), (cot_h, cot), (tn_h, tn))
    finish_all([begin(a, b, sems.at[k]) for k, (a, b) in enumerate(pairs)])

    def step(p, carry):
        at = pl.ds(pl.multiple_of(p * LANES, LANES), LANES)
        g, up = gate[:, at], cot[:, at].astype(F32)
        o = dot(owt[...], tn[:, at])
        tile = (g * o).T.astype(BF16)
        cols = update.shape[1]
        update[p] = tile[:cols]
        update[half + p] = tile[cols:]
        og[:, at] = (up * g).astype(BF16)
        gg[:, at] = (up * o * g * (1.0 - g)).astype(BF16)
        return carry

    lax.fori_loop(0, half, step, 0, unroll=2)
    stored = begin(gg, gg_h, sems.at[len(pairs)])
    early[0] = dot(nt[...], gg[...], NT)
    early[1] = dot(tn[...], og[...], NT)
    norms[0:1] = fold(sums[0])
    norms[1:2] = fold(sums[1])
    stored.wait()


def combine(half, hidden, scr, coef, side, p):
    at = pl.ds(pl.multiple_of(p * LANES, LANES), LANES)
    part = scr[side, pl.ds(p, hidden, stride=half + 1), :]
    value = (part * coef[2 * side, :, at].astype(F32)).astype(BF16)
    slope = (part * coef[2 * side + 1, :, at].astype(F32)).astype(BF16)
    return jnp.concatenate([value, slope], axis=0)


def finish(half, hidden, recv, coef_h, nt, early, parts, coef, comb, scr, total, sems):
    size = nt.shape[1] // GROUPS
    fetched = []
    for g in range(GROUPS):
        at = span(g, size)
        fetched.append(begin(coef_h.at[:, :, at], coef.at[:, :, at], sems.at[g]))
    for side in (0, 1):
        unpack(half, recv, scr.at[side], side)

    def step(p, carry):
        at = pl.ds(pl.multiple_of(p * LANES, LANES), LANES)
        for side in (0, 1):
            comb[side, :, at] = combine(half, hidden, scr, coef, side, p)
        return carry

    for g in range(GROUPS):
        fetched[g].wait()
        count = half // GROUPS
        lax.fori_loop(g * count, (g + 1) * count, step, 0, unroll=8)
        here = slice(g * size, (g + 1) * size)
        for side in (0, 1):
            part = dot(nt[:, here], comb[side, :, here], NT)
            total[side] = part if g == 0 else total[side] + part
    c = nt.shape[0]
    base = 5 * c + hidden
    for side in (0, 1):
        grad = total[side]
        parts[2 * side * c : (2 * side + 1) * c] = grad[:, :hidden].astype(BF16)
        parts[(2 * side + 1) * c : (2 * side + 2) * c] = grad[:, hidden:].astype(BF16)
    parts[4 * c : 5 * c] = early[0].astype(BF16)
    parts[5 * c : base] = early[1].astype(BF16)
    if parts.shape[0] > base:
        parts[base:] = jnp.zeros((parts.shape[0] - base, LANES), BF16)


def close(half, hidden, recv, coef_h, gg_h, hat_h, scale, gain, lw, rw, gw, early_norms, grad_pair, pairs, coef, gg, hat, scr, sums, gb, sems):
    size = gg.shape[1] // GROUPS
    fetched = []
    for g in range(GROUPS):
        at = span(g, size)
        fetched.append(begin(coef_h.at[:, :, at], coef.at[:, :, at], sems.at[3 * g]))
        fetched.append(begin(gg_h.at[:, at], gg.at[:, at], sems.at[3 * g + 1]))
        fetched.append(begin(hat_h.at[:, at], hat.at[:, at], sems.at[3 * g + 2]))
    for side in (0, 1):
        unpack(half, recv, scr.at[side], side)
    gb[...] = column(gain[...])
    sums[...] = jnp.zeros_like(sums)
    cols = grad_pair.shape[1]

    def step(p, carry):
        at = pl.ds(pl.multiple_of(p * LANES, LANES), LANES)
        h = hat[:, at]
        ng = dot(gw[...], gg[:, at])
        for side, w in ((0, lw), (1, rw)):
            ng = ng + dot(w[...], combine(half, hidden, scr, coef, side, p))
        sums[0] += ng * h
        sums[1] += ng
        q = ng * gb[...]
        back = q - jnp.mean(q, axis=0, keepdims=True)
        back = back - h * jnp.mean(q * h, axis=0, keepdims=True)
        tile = (scale[0:1, at] * back).T.astype(BF16)
        grad_pair[p] = tile[:cols]
        grad_pair[half + p] = tile[cols:]
        return carry

    for g in range(GROUPS):
        finish_all(fetched[3 * g : 3 * g + 3])
        count = half // GROUPS
        lax.fori_loop(g * count, (g + 1) * count, step, 0, unroll=2)
    exact = jnp.concatenate([fold(sums[0]), fold(sums[1]), early_norms[0:2]], axis=0)
    high = exact.astype(BF16)
    pairs[...] = jnp.concatenate([high, (exact - high.astype(F32)).astype(BF16)], axis=0)


def add_up(scale, recv, pairs, send):
    n_dev, share, _ = recv.shape
    mine = (scale * jnp.sum(recv[...].astype(F32), axis=0)).astype(BF16)
    own = pairs[...]
    for d in range(n_dev):
        send[d, :share] = mine
        send[d, share:] = own


def deliver(scale, recv, left, right, gating, output, norms, flat):
    c = left.shape[0]
    n_dev, share = recv.shape[0], recv.shape[1] - 8
    total = jnp.zeros((8, LANES), F32)
    for d in range(n_dev):
        flat[d * share : (d + 1) * share] = recv[d, :share].astype(F32)
        total = total + recv[d, share:].astype(F32)
    for k, out in ((0, left), (2, right)):
        out[:, :LANES] = flat[k * c : (k + 1) * c]
        out[:, LANES:] = flat[(k + 1) * c : (k + 2) * c]
    gating[...] = flat[4 * c : 5 * c]
    output[...] = flat[5 * c : 5 * c + output.shape[0]]
    norms[...] = scale * (total[0:4] + total[4:8])


def per_device(
    pair,
    cotangent,
    length,
    norm_gain,
    norm_bias,
    left_weight,
    right_weight,
    gate_weight,
    out_gain,
    out_bias,
    out_weight,
):
    n_row = lax.axis_size("row")
    n_col = lax.axis_size("col")
    n_dev = n_row * n_col
    rows_dev, cols_dev, c = pair.shape
    tokens = rows_dev * n_row
    hidden = out_weight.shape[0]
    own = hidden // n_dev
    half = rows_dev * cols_dev // LANES
    wide = half * LANES
    per = own * half
    assert 2 * cols_dev == LANES and rows_dev == 2 * half and c == LANES and hidden == LANES
    gain, bias = norm_gain[None], norm_bias[None]
    o_gain, o_bias = out_gain[None], out_bias[None]
    vm, dma = pltpu.VMEM, pltpu.SemaphoreType.DMA
    sq = (c, LANES)
    rows = hidden * (half + 1) + 2 * half

    send, nt = call(
        functools.partial(project, half, hidden),
        (SMEM,) + (HBM,) * 5,
        [((n_dev, 2, per, LANES), BF16, VMEM), ((c, wide), BF16, VMEM)],
        [vm(pair.shape, BF16), vm((1, c), F32), vm((1, c), F32), vm((2, c, 2 * hidden), BF16)]
        + [vm((2, 2 * hidden, c), BF16), vm((2,) + sq, F32), vm((rows, LANES), F32)]
        + [vm((rows, LANES), F32), dma((4 + 2 * GROUPS,))],
        "project", 300 * 10**6, 3 * 2**20,
    )(length, pair, gain, bias, left_weight, right_weight)
    both = exchange(send)
    gate, cot, coef, hat, scale = call(
        functools.partial(prepare, half, hidden),
        (SMEM,) + (VMEM,) * 6,
        [((c, wide), F32, VMEM), ((c, wide), BF16, VMEM), ((4, hidden, wide), BF16, VMEM)]
        + [((c, wide), F32, VMEM), ((8, wide), F32, VMEM)],
        [vm((2, 2 * hidden, c), BF16), vm((c, c), BF16)],
        "prepare", 400 * 10**6, 9 * 2**20,
    )(length, pair, cotangent, nt, left_weight, right_weight, gate_weight)
    send, left, right = call(
        functools.partial(multiply, n_row, n_col, half),
        (VMEM,),
        [((n_dev, per, LANES), BF16, HBM)] + [((own, tokens, tokens), BF16, VMEM)] * 2,
        [vm((own, tokens, tokens), F32), vm((n_dev, per, LANES), BF16), dma((own,))],
        "multiply", 200 * 10**6, 3 * 2**20,
    )(both)
    tri = exchange(send)
    send, tn, sums = call(
        functools.partial(middle, half, hidden),
        (VMEM, HBM, HBM, VMEM, VMEM, VMEM),
        [((n_dev, per, LANES), BF16, VMEM), ((c, wide), BF16, HBM), ((2,) + sq, F32, VMEM)],
        [vm((c, wide), F32)] + [vm((c, wide), BF16)] * 2 + [vm((rows, LANES), F32)]
        + [vm((2,) + sq, F32), dma((2 * GROUPS,)), dma((GROUPS,))],
        "middle", 200 * 10**6, 6 * 2**20,
    )(tri, gate, cot, o_gain, o_bias, out_weight)
    grad = exchange(send)
    update, gg, early, early_norms = call(
        functools.partial(settle, half),
        (HBM,) * 3 + (VMEM,) * 3,
        [((rows_dev, cols_dev, c), BF16, VMEM), ((c, wide), BF16, HBM)]
        + [((2,) + sq, F32, VMEM), ((8, LANES), F32, VMEM)],
        [vm((c, wide), F32)] + [vm((c, wide), BF16)] * 4 + [vm((c, hidden), BF16), dma((4,))],
        "settle", 200 * 10**6, 4 * 2**20,
    )(gate, cot, tn, nt, sums, out_weight)
    (send,) = call(
        functools.partial(multiply_back, n_row, n_col, half),
        (VMEM,) * 3,
        [((n_dev, 2, per, LANES), BF16, HBM)],
        [vm((own, tokens, tokens), BF16), vm((own, 2, tokens, tokens), F32)]
        + [vm((n_dev, 2, per, LANES), BF16), dma((own,))],
        "multiply_back", 300 * 10**6, 3 * 2**20,
    )(grad, left, right)
    back = exchange(send)
    share = -(-(5 * c + hidden) // (n_dev * 8)) * 8
    (parts,) = call(
        functools.partial(finish, half, hidden),
        (VMEM, HBM, VMEM, VMEM),
        [((n_dev * share, LANES), BF16, VMEM)],
        [vm((4, hidden, wide), BF16), vm((2, 2 * hidden, wide), BF16), vm((2, rows, LANES), F32)]
        + [vm((2, c, 2 * hidden), F32), dma((GROUPS,))],
        "finish", 300 * 10**6, 8 * 2**20,
    )(back, coef, nt, early)
    summed = exchange(parts.reshape(n_dev, share, LANES))
    grad_pair, pairs = call(
        functools.partial(close, half, hidden),
        (VMEM,) + (HBM,) * 3 + (VMEM,) * 6,
        [((rows_dev, cols_dev, c), BF16, VMEM), ((8, LANES), BF16, VMEM)],
        [vm((4, hidden, wide), BF16), vm((c, wide), BF16), vm((c, wide), F32)]
        + [vm((2, rows, LANES), F32), vm((2,) + sq, F32), vm(sq, F32), dma((3 * GROUPS,))],
        "close", 300 * 10**6, 6 * 2**20,
    )(back, coef, gg, hat, scale, gain, left_weight, right_weight, gate_weight, early_norms)
    (send,) = call(
        functools.partial(add_up, 1.0 / tokens),
        (VMEM, VMEM),
        [((n_dev, share + 8, LANES), BF16, VMEM)],
        [],
        "add_up", 10**6, 2**19,
    )(summed, pairs)
    grads = call(
        functools.partial(deliver, 1.0 / tokens),
        (VMEM,),
        [((c, 2 * hidden), F32, VMEM)] * 2
        + [((c, c), F32, VMEM), ((hidden, c), F32, VMEM), ((4, c), F32, VMEM)],
        [vm((n_dev * share, LANES), F32)],
        "deliver", 10**6, 2**20,
    )(exchange(send))
    return (update, grad_pair) + tuple(grads)


def solution(mesh):
    return jax.shard_map(
        per_device,
        mesh=mesh,
        in_specs=(P("row", "col", None), P("row", "col", None)) + (P(),) * 9,
        out_specs=(P("row", "col", None), P("row", "col", None), P(), P(), P(), P(), P()),
        check_vma=False,
    )
```
